32 devices in a mesh: dp: 8 (over z, y), mp: 4 (over x, core).
Axes of the slice: x: 2, y: 2, z: 4, core: 2. Of those that a mesh axis runs over, the one named last changes fastest.
Arguments:
- tokens: bfloat16 [192, 196, 768], P('dp'), may hold values from -6 to 6
- cotangent: bfloat16 [192, 196, 768], P('dp'), may hold values from -6 to 6
- counts: int32 [8], replicated, may hold values from 1 to 24, as said below
- vec_params: float32 [5, 768], replicated, as said below
- vec_moments: float32 [2, 5, 768], replicated, as said below
- token_w1: float32 [196, 384], replicated, may hold values from -0.4375 to 0.4375
- token_w1_moments: float32 [2, 196, 384], replicated, as said below
- token_w2: float32 [384, 196], replicated, may hold values from -0.3125 to 0.3125
- token_w2_moments: float32 [2, 384, 196], replicated, as said below
- token_bias: float32 [580], replicated, may hold values from -0.5 to 0.5
- token_bias_moments: float32 [2, 580], replicated, as said below
- chan_w1: float32 [768, 3072], P(None, 'mp'), may hold values from -0.21875 to 0.21875
- chan_w1_moments: float32 [2, 768, 3072], P(None, None, 'mp'), as said below
- chan_b1: float32 [3072], P('mp'), may hold values from -0.5 to 0.5
- chan_b1_moments: float32 [2, 3072], P(None, 'mp'), as said below
- chan_w2: float32 [3072, 768], P('mp'), may hold values from -0.109375 to 0.109375
- chan_w2_moments: float32 [2, 3072, 768], P(None, 'mp'), as said below
Outputs:
- output: bfloat16 [192, 196, 768], P('dp')
- input_grad: bfloat16 [192, 196, 768], P('dp')
- vec_moments_new: float32 [2, 5, 768], replicated
- token_w1_new: float32 [196, 384], replicated
- token_w1_moments_new: float32 [2, 196, 384], replicated
- token_w2_new: float32 [384, 196], replicated
- token_w2_moments_new: float32 [2, 384, 196], replicated
- token_bias_new: float32 [580], replicated
- token_bias_moments_new: float32 [2, 580], replicated
- chan_w1_new: float32 [768, 3072], P(None, 'mp')
- chan_w1_moments_new: float32 [2, 768, 3072], P(None, None, 'mp')
- chan_b1_new: float32 [3072], P('mp')
- chan_b1_moments_new: float32 [2, 3072], P(None, 'mp')
- chan_w2_new: float32 [3072, 768], P('mp')
- chan_w2_moments_new: float32 [2, 3072, 768], P(None, 'mp')
The draws below stay inside these ranges and needn't reach their ends.
Inputs may be any that keep to these rules, and one draw needn't show every extreme that they name: `counts`: each index of dp holds 1 to 24 live images, the first ones of its slots; some index holds 24. `vec_params`: rows 0 and 2 lie between 0.5 and 1.5. `chan_w1_moments`: the second moments (index 1) are positive. `chan_w2_moments`: the second moments (index 1) are positive. `chan_b1_moments`: the second moments (index 1) are positive. `token_w1_moments`: the second moments (index 1) are positive. `token_w2_moments`: the second moments (index 1) are positive. `token_bias_moments`: the second moments (index 1) are positive. `vec_moments`: the second moments (index 1) are positive.
All inputs are finite; a program needn't handle non-finite values.
Results may differ from the reference program's by a relative error of at most 0.012.
Values may be sent and summed in bfloat16 or wider, within the bound.
No kernel may reach another device: no remote copies, remote signals or barrier semaphores. Data moves between devices by JAX's collectives and lax.ppermute only.
A program may use at most 320 MiB of HBM per device.

```python
import math
import jax
import jax.numpy as jnp
from jax import lax

C = 768
S = 196
DS = 384
DC = 3072
IMG_DEV = 24
STEP = 4
IMAGES = 192
N_DP = 8
N_MP = 4


def typical_scale():
    return math.sqrt(1.0 / (0.6 * IMAGES))


def moment_pair(key, shape, size):
    first_key, second_key = jax.random.split(key)
    first = size * jnp.clip(jax.random.normal(first_key, shape, jnp.float32), -3.0, 3.0)
    second = size * size * jnp.exp(jax.random.uniform(second_key, shape, jnp.float32, 0.0, math.log(4.0)))
    return jnp.stack([first, second])


def draw_counts(key, part):
    first_key, second_key = jax.random.split(key)
    drawn = jax.random.randint(first_key, (N_DP,), 1, IMG_DEV + 1)
    full_index = jax.random.randint(second_key, (), 0, N_DP)
    return jnp.where(jnp.arange(N_DP) == full_index, IMG_DEV, drawn).astype(jnp.int32)


def draw_vec_params(key, part):
    first_key, second_key = jax.random.split(key)
    gains = jax.random.uniform(first_key, (5, C), jnp.float32, 0.5, 1.5)
    shifts = 0.3 * jnp.clip(jax.random.normal(second_key, (5, C), jnp.float32), -5.0, 5.0)
    row_ids = jnp.arange(5)[:, None]
    return jnp.where((row_ids == 0) | (row_ids == 2), gains, shifts)


def draw_vec_moments(key, part):
    return moment_pair(key, (5, C), 0.8 * math.sqrt(S) * typical_scale())


def draw_token_w1_moments(key, part):
    return moment_pair(key, (S, DS), 0.6 * math.sqrt(C) * typical_scale())


def draw_token_w2_moments(key, part):
    return moment_pair(key, (DS, S), 0.8 * math.sqrt(C) * typical_scale())


def draw_token_bias_moments(key, part):
    return moment_pair(key, (DS + S,), 0.8 * math.sqrt(C) * typical_scale())


def draw_chan_w1_moments(key, part):
    return moment_pair(key, (C, DC), 0.35 * math.sqrt(S) * typical_scale())


def draw_chan_b1_moments(key, part):
    return moment_pair(key, (DC,), 0.35 * math.sqrt(S) * typical_scale())


def draw_chan_w2_moments(key, part):
    return moment_pair(key, (DC, C), 0.65 * math.sqrt(S) * typical_scale())


def level_of(own_key, shape, pieces, low, top_value):
    factor_of = 1.0
    for axis_at, shards_of in pieces:
        steps = jax.random.uniform(jax.random.fold_in(jax.random.fold_in(own_key, 6), axis_at), (shards_of,), jnp.float32, low / len(pieces), top_value / len(pieces))
        factor_of = factor_of * jnp.repeat(jnp.exp(steps), shape[axis_at] // shards_of).reshape((-1,) + (1,) * (len(shape) - 1 - axis_at))
    return factor_of


def gaussian(own_key, dims, scale, reach, pieces=(), kind=jnp.bfloat16):
    level = level_of(own_key, dims, pieces, -0.22, 0.18) if pieces else 1.0
    array = jax.random.normal(own_key, dims, jnp.float32) * scale * level
    return jnp.minimum(jnp.maximum(array, -reach), reach).astype(kind)


def setup_inputs(seed: int = 0) -> dict:
    key_list = jax.random.split(jax.random.key(seed), 18)
    return {
        "tokens": gaussian(key_list[0], (IMAGES, S, C), 1.0, 6.0, ((0, 8),)),
        "cotangent": gaussian(key_list[1], (IMAGES, S, C), 1.0, 6.0, ((0, 8),)),
        "counts": draw_counts(jax.random.fold_in(key_list[17], 71), 0),
        "vec_params": draw_vec_params(jax.random.fold_in(key_list[17], 71), 0),
        "vec_moments": draw_vec_moments(jax.random.fold_in(key_list[17], 71), 0),
        "token_w1": gaussian(key_list[5], (S, DS), S ** -0.5, 0.4375, (), jnp.float32),
        "token_w1_moments": draw_token_w1_moments(jax.random.fold_in(key_list[17], 71), 0),
        "token_w2": gaussian(key_list[7], (DS, S), DS ** -0.5, 0.3125, (), jnp.float32),
        "token_w2_moments": draw_token_w2_moments(jax.random.fold_in(key_list[17], 71), 0),
        "token_bias": gaussian(key_list[9], (DS + S,), 0.1, 0.5, (), jnp.float32),
        "token_bias_moments": draw_token_bias_moments(jax.random.fold_in(key_list[17], 71), 0),
        "chan_w1": gaussian(key_list[11], (C, DC), C ** -0.5, 0.21875, ((1, 4),), jnp.float32),
        "chan_w1_moments": draw_chan_w1_moments(jax.random.fold_in(key_list[17], 71), 0),
        "chan_b1": gaussian(key_list[13], (DC,), 0.1, 0.5, ((0, 4),), jnp.float32),
        "chan_b1_moments": draw_chan_b1_moments(jax.random.fold_in(key_list[17], 71), 0),
        "chan_w2": gaussian(key_list[15], (DC, C), DC ** -0.5, 0.109375, ((0, 4),), jnp.float32),
        "chan_w2_moments": draw_chan_w2_moments(jax.random.fold_in(key_list[17], 71), 0),
    }


@jax.custom_vjp
def low(v):
    return lax.optimization_barrier(v.astype(jnp.bfloat16)).astype(jnp.float32)

@jax.custom_vjp
def low_back(v):
    return v

def low_keep(v):
    return (low(v), None)

def low_pass(kept, grad):
    return (grad,)

def back_keep(v):
    return (v, None)

def back_low(kept, grad):
    return (low(grad),)
low.defvjp(low_keep, low_pass)
low_back.defvjp(back_keep, back_low)
highest = lax.Precision.HIGHEST
norm_eps = 1e-06
learn_rate = 0.02
decay_rate = 0.5
weight_decay = 0.05
adam_eps = 1e-08

def gelu_exact(values):
    return jax.nn.gelu(values, approximate=False)

def layer_norm(values, gain, shift):
    center = values - lax.optimization_barrier(jnp.mean(values, axis=-1, keepdims=True))
    inv_std = lax.rsqrt(lax.optimization_barrier(jnp.mean(center * center, axis=-1, keepdims=True)) + norm_eps)
    return center * inv_std * gain + shift

def forward(inputs, weights):
    vec_params, token_w1, token_w2, token_bias, chan_w1, chan_b1, chan_w2 = weights
    normed = low(layer_norm(inputs, vec_params[0], vec_params[1]))
    token_pre = low_back(jnp.einsum('bsc,sk->bck', normed, low(token_w1), precision=highest) + token_bias[:DS])
    token_act = low(gelu_exact(token_pre))
    token_out = low_back(jnp.einsum('bck,ks->bsc', token_act, low(token_w2), precision=highest) + token_bias[DS:][:, None])
    mixed = inputs + token_out
    second = low(layer_norm(mixed, vec_params[2], vec_params[3]))
    chan_pre = low_back(jnp.einsum('bsc,ch->bsh', second, low(chan_w1), precision=highest) + chan_b1)
    chan_act = low(gelu_exact(chan_pre))
    per_device = DC // N_MP
    summed = jnp.zeros(mixed.shape, jnp.float32)
    for column in range(N_MP):
        start = column * per_device
        summed = summed + low(jnp.einsum('bsh,hc->bsc', chan_act[:, :, start:start + per_device], low(chan_w2[start:start + per_device]), precision=highest))
    return mixed + low_back(summed + vec_params[4])

def adam_update(weight, moments, grads):
    first = decay_rate * moments[0] + (1.0 - decay_rate) * grads
    second = decay_rate * moments[1] + (1.0 - decay_rate) * grads * grads
    correct = 1.0 - decay_rate ** STEP
    step_size = first / correct / (jnp.sqrt(second / correct) + adam_eps)
    return (weight - learn_rate * (step_size + weight_decay * weight), jnp.stack([first, second]))

def reference(tokens, cotangent, counts, vec_params, vec_moments, token_w1, token_w1_moments, token_w2, token_w2_moments, token_bias, token_bias_moments, chan_w1, chan_w1_moments, chan_b1, chan_b1_moments, chan_w2, chan_w2_moments):
    weights = (vec_params, token_w1, token_w2, token_bias, chan_w1, chan_b1, chan_w2)
    image_ids = jnp.arange(IMAGES, dtype=jnp.int32)
    live = image_ids % IMG_DEV < counts[image_ids // IMG_DEV]
    total = jnp.sum(counts).astype(jnp.float32)
    scales = jnp.where(live, 1.0, 0.0).astype(jnp.float32) / total
    blocks = (tokens.reshape(N_DP, IMG_DEV, S, C), cotangent.reshape(N_DP, IMG_DEV, S, C), scales.reshape(N_DP, IMG_DEV))

    def one_block(carry, block):
        inputs, back, weight_rows = block
        result, pullback = jax.vjp(forward, inputs.astype(jnp.float32), weights)
        grad_inputs, grad_weights = pullback(back.astype(jnp.float32) * weight_rows[:, None, None])
        carry = jax.tree.map(lambda total_grad, part_grad: total_grad + part_grad, carry, grad_weights)
        return (carry, (result.astype(jnp.bfloat16), grad_inputs.astype(jnp.bfloat16)))
    zero_grads = jax.tree.map(jnp.zeros_like, weights)
    grads, (outputs, input_grads) = lax.scan(one_block, zero_grads, blocks)
    vec_new, vec_moments_new = adam_update(vec_params, vec_moments, grads[0])
    token_w1_new, token_w1_moments_new = adam_update(token_w1, token_w1_moments, grads[1])
    token_w2_new, token_w2_moments_new = adam_update(token_w2, token_w2_moments, grads[2])
    token_bias_new, token_bias_moments_new = adam_update(token_bias, token_bias_moments, grads[3])
    chan_w1_new, chan_w1_moments_new = adam_update(chan_w1, chan_w1_moments, grads[4])
    chan_b1_new, chan_b1_moments_new = adam_update(chan_b1, chan_b1_moments, grads[5])
    chan_w2_new, chan_w2_moments_new = adam_update(chan_w2, chan_w2_moments, grads[6])
    return (outputs.reshape(IMAGES, S, C), input_grads.reshape(IMAGES, S, C), vec_moments_new, token_w1_new, token_w1_moments_new, token_w2_new, token_w2_moments_new, token_bias_new, token_bias_moments_new, chan_w1_new, chan_w1_moments_new, chan_b1_new, chan_b1_moments_new, chan_w2_new, chan_w2_moments_new)
```

```python
import functools
import jax
import jax.numpy as jnp
from jax import lax
from jax.experimental import pallas as pl
from jax.experimental.pallas import tpu as pltpu
from jax.sharding import PartitionSpec as P

STEP = 4
norm_eps = 1e-06
learn_rate = 0.02
decay_rate = 0.5
weight_decay = 0.05
adam_eps = 1e-08

bf = jnp.bfloat16
f32 = jnp.float32
VMEM_LIMIT = 60 << 20


def sds(shape, dtype):
    return jax.ShapeDtypeStruct(shape, dtype)


def dot_nn(a, b):
    return jnp.dot(a, b, preferred_element_type=f32)


def dot_nt(a, b):
    return lax.dot_general(a, b, (((1,), (1,)), ((), ())), preferred_element_type=f32)


def dot_tn(a, b):
    return lax.dot_general(a, b, (((0,), (0,)), ((), ())), preferred_element_type=f32)


def gelu_pair(v):
    cdf = 0.5 * (1.0 + lax.erf(v * 0.7071067811865476))
    pdf = jnp.exp(-0.5 * v * v) * 0.3989422804014327
    return v * cdf, cdf + v * pdf


def norm_parts(values):
    center = values - jnp.mean(values, axis=-1, keepdims=True)
    inv_std = lax.rsqrt(jnp.mean(center * center, axis=-1, keepdims=True) + norm_eps)
    return center * inv_std, inv_std


def row_mean(values):
    return jnp.mean(values, axis=-1, keepdims=True)


def col_sum(values):
    return jnp.sum(values, axis=0, keepdims=True)


def token_fwd_kernel(
    rw_ref, x_ref, ct_ref, w1t_ref, w2t_ref, b1_ref, b2_ref, vec_ref,
    mixed_ref, second_ref, low_ref, act_ref, slope_ref,
):
    b = pl.program_id(0)
    x = x_ref[0].astype(f32)
    hat1, _ = norm_parts(x)
    normed = (hat1 * vec_ref[0:1] + vec_ref[1:2]).astype(bf)
    act, slope = gelu_pair(dot_nn(w1t_ref[...], normed) + b1_ref[...])
    act = act.astype(bf)
    act_ref[0] = act
    slope_ref[0] = slope.astype(bf)
    mixed = x + (dot_nn(w2t_ref[...], act) + b2_ref[...])
    mixed_ref[0] = mixed
    hat2, _ = norm_parts(mixed)
    second_ref[0] = (hat2 * vec_ref[2:3] + vec_ref[3:4]).astype(bf)
    low_ref[0] = (ct_ref[0].astype(f32) * rw_ref[b]).astype(bf)


def image_spec(*shape):
    return pl.BlockSpec((1,) + shape, lambda b: (b, 0, 0))


def whole_spec(*shape):
    return pl.BlockSpec(shape, lambda b: (0,) * len(shape))


SMEM_SPEC = pl.BlockSpec(memory_space=pltpu.SMEM)
VMEM_SPEC = pl.BlockSpec(memory_space=pltpu.VMEM)


def token_fwd(rw, x, ct, w1t, w2t, b1, b2, vec):
    n, s, c = x.shape
    k = w1t.shape[0]
    return pl.pallas_call(
        token_fwd_kernel,
        grid=(n,),
        in_specs=[SMEM_SPEC, image_spec(s, c), image_spec(s, c)]
        + [whole_spec(*a.shape) for a in (w1t, w2t, b1, b2, vec)],
        out_specs=[image_spec(s, c)] * 3 + [image_spec(k, c)] * 2,
        out_shape=[sds((n, s, c), f32), sds((n, s, c), bf), sds((n, s, c), bf)]
        + [sds((n, k, c), bf)] * 2,
        compiler_params=pltpu.CompilerParams(vmem_limit_bytes=VMEM_LIMIT),
        cost_estimate=pl.CostEstimate(
            flops=n * s * c * k * 4, transcendentals=n * k * c * 2, bytes_accessed=n * c * (s * 10 + k * 4)
        ),
        name="token_fwd",
    )(rw, x, ct, w1t, w2t, b1, b2, vec)


def chan_kernel(s_ref, g_ref, w_ref, b1_ref, out_ref, sg_ref, dw_ref, db1_ref):
    c = s_ref.shape[1]
    s = s_ref[...]
    g = g_ref[...]
    w1 = w_ref[:c]
    w2 = w_ref[c:]
    act, slope = gelu_pair(dot_nn(s, w1) + b1_ref[...])
    act = act.astype(bf)
    pre_grad = (dot_nt(g, w2) * slope).astype(bf)
    out_ref[...] = dot_nn(act, w2).astype(bf)
    sg_ref[...] = dot_nt(pre_grad, w1).astype(bf)
    dw_ref[c:] = dot_tn(act, g).astype(bf)
    dw_ref[:c] = dot_tn(s, pre_grad).astype(bf)
    db1_ref[...] = col_sum(pre_grad.astype(f32))


def chan(s, g, w, b1):
    r, c = s.shape
    h = b1.shape[1]
    return pl.pallas_call(
        chan_kernel,
        in_specs=[VMEM_SPEC] * 4,
        out_specs=[VMEM_SPEC] * 4,
        out_shape=[sds((r, c), bf), sds((r, c), bf), sds((c + h, c), bf), sds((1, h), f32)],
        compiler_params=pltpu.CompilerParams(vmem_limit_bytes=VMEM_LIMIT),
        cost_estimate=pl.CostEstimate(
            flops=12 * r * c * h, transcendentals=2 * r * h, bytes_accessed=8 * r * c + 8 * c * h
        ),
        name="chan",
    )(s, g, w, b1)


def out_kernel(mixed_ref, p0, p1, p2, p3, vec_ref, out_ref):
    total = (p0[0].astype(f32) + p1[0].astype(f32)) + (p2[0].astype(f32) + p3[0].astype(f32))
    out_ref[0] = (mixed_ref[0] + (total + vec_ref[4:5])).astype(bf)


def make_output(mixed, parts, vec):
    n, s, c = mixed.shape
    return pl.pallas_call(
        out_kernel,
        grid=(n,),
        in_specs=[image_spec(s, c)] * 5 + [whole_spec(*vec.shape)],
        out_specs=image_spec(s, c),
        out_shape=sds((n, s, c), bf),
        cost_estimate=pl.CostEstimate(flops=n * s * c * 6, transcendentals=0, bytes_accessed=n * s * c * 14),
        name="make_output",
    )(mixed, *parts, vec)


def token_bwd_kernel(
    rw_ref, x_ref, ct_ref, mixed_ref, sg0, sg1, sg2, sg3, act_ref, slope_ref, w1_ref, w2_ref, vec_ref,
    ig_ref, grads_ref,
):
    b = pl.program_id(0)
    s, k = w1_ref.shape
    x = x_ref[0].astype(f32)
    hat1, r1 = norm_parts(x)
    normed = (hat1 * vec_ref[0:1] + vec_ref[1:2]).astype(bf)
    hat2, r2 = norm_parts(mixed_ref[0])
    sg = (sg0[0].astype(f32) + sg1[0].astype(f32)) + (sg2[0].astype(f32) + sg3[0].astype(f32))
    grad_out = ct_ref[0].astype(f32) * rw_ref[b]
    grad_low = grad_out.astype(bf).astype(f32)
    h2 = sg * vec_ref[2:3]
    mixed_grad = grad_out + r2 * (h2 - row_mean(h2) - hat2 * row_mean(h2 * hat2))
    token_grad = mixed_grad.astype(bf)
    pre_grad = (dot_nn(w2_ref[...], token_grad) * slope_ref[0].astype(f32)).astype(bf)
    w1_grad = dot_nt(normed, pre_grad)
    w2_grad = dot_nt(token_grad, act_ref[0])
    normed_grad = dot_nn(w1_ref[...], pre_grad)
    h1 = normed_grad * vec_ref[0:1]
    ig = mixed_grad + r1 * (h1 - row_mean(h1) - hat1 * row_mean(h1 * hat1))
    ig_ref[0] = ig.astype(bf)
    ones = jnp.ones((8, x.shape[1]), bf)
    in_row = dot_nt(ones, pre_grad)[0:1]
    out_row = dot_nt(ones, token_grad)[0:1]
    rows = [
        col_sum(normed_grad * hat1), col_sum(normed_grad), col_sum(sg * hat2), col_sum(sg), col_sum(grad_low),
    ]

    @pl.when(b == 0)
    def _():
        grads_ref[...] = jnp.zeros_like(grads_ref)

    grads_ref[0:s, 0:k] += w1_grad
    grads_ref[0:s, k : 2 * k] += w2_grad
    for i, row in enumerate(rows):
        grads_ref[s + i : s + i + 1, :] += row
    grads_ref[s + 5 : s + 6, 0:k] += in_row
    grads_ref[s + 5 : s + 6, k : k + s] += out_row


def token_bwd(rw, x, ct, mixed, sgs, act, slope, w1, w2, vec):
    n, s, c = x.shape
    k = w1.shape[1]
    return pl.pallas_call(
        token_bwd_kernel,
        grid=(n,),
        in_specs=[SMEM_SPEC] + [image_spec(s, c)] * 7 + [image_spec(k, c)] * 2
        + [whole_spec(*a.shape) for a in (w1, w2, vec)],
        out_specs=[image_spec(s, c), whole_spec(s + 8, c)],
        out_shape=[sds((n, s, c), bf), sds((s + 8, c), f32)],
        compiler_params=pltpu.CompilerParams(vmem_limit_bytes=VMEM_LIMIT),
        cost_estimate=pl.CostEstimate(
            flops=n * s * c * k * 8, transcendentals=0, bytes_accessed=n * c * (s * 18 + k * 4)
        ),
        name="token_bwd",
    )(rw, x, ct, mixed, *sgs, act, slope, w1, w2, vec)


def gather_kernel(order_ref, a_ref, b_ref, c_ref, d_ref, o_ref):
    refs = (a_ref, b_ref, c_ref, d_ref)
    for j in range(4):

        @pl.when(order_ref[0] == j)
        def _():
            images = jnp.concatenate([refs[j ^ k][...] for k in range(4)], axis=0)
            o_ref[...] = jnp.swapaxes(images, 0, 1)


def gather_images(order, parts, s_true, block=40):
    n, s, c = parts[0].shape
    out = pl.pallas_call(
        gather_kernel,
        grid=(s // block,),
        in_specs=[SMEM_SPEC] + [pl.BlockSpec((n, block, c), lambda i: (0, i, 0))] * 4,
        out_specs=pl.BlockSpec((block, 4 * n, c), lambda i: (i, 0, 0)),
        out_shape=sds((s_true, 4 * n, c), bf),
        compiler_params=pltpu.CompilerParams(vmem_limit_bytes=VMEM_LIMIT),
        cost_estimate=pl.CostEstimate(flops=0, transcendentals=0, bytes_accessed=n * s * c * 16),
        name="gather_images",
    )(order, *parts)
    return jnp.swapaxes(out, 0, 1)


def swap(values, axis, size, bit):
    return lax.ppermute(values, axis, [(i, i ^ bit) for i in range(size)])


def halve(values, axis, size, bit):
    upper = (lax.axis_index(axis) // bit) % 2
    half = values.shape[0] // 2
    send = lax.dynamic_slice_in_dim(values, (1 - upper) * half, half, 0)
    keep = lax.dynamic_slice_in_dim(values, upper * half, half, 0)
    got = swap(send, axis, size, bit)
    return (keep.astype(f32) + got.astype(f32)).astype(bf)


def double(values, axis, size, bit):
    upper = (lax.axis_index(axis) // bit) % 2
    got = swap(values, axis, size, bit)
    return jnp.where(
        upper == 0, jnp.concatenate([values, got], axis=0), jnp.concatenate([got, values], axis=0)
    )


def add_swapped(values, axis, size, bit):
    got = swap(values, axis, size, bit)
    return (values.astype(f32) + got.astype(f32)).astype(bf)


def bits_of(size):
    return [1 << b for b in range(size.bit_length() - 1)]


def adam_update(weight, moments, grads):
    first = decay_rate * moments[0] + (1.0 - decay_rate) * grads
    second = decay_rate * moments[1] + (1.0 - decay_rate) * grads * grads
    correct = 1.0 - decay_rate**STEP
    step_size = first / correct / (jnp.sqrt(second / correct) + adam_eps)
    return (weight - learn_rate * (step_size + weight_decay * weight), jnp.stack([first, second]))


def new_moments(moments, grads):
    first = decay_rate * moments[0] + (1.0 - decay_rate) * grads
    second = decay_rate * moments[1] + (1.0 - decay_rate) * grads * grads
    return jnp.stack([first, second])


def shards(
    n_dp,
    tokens,
    cotangent,
    counts,
    vec_params,
    vec_moments,
    token_w1,
    token_w1_moments,
    token_w2,
    token_w2_moments,
    token_bias,
    token_bias_moments,
    chan_w1,
    chan_w1_moments,
    chan_b1,
    chan_b1_moments,
    chan_w2,
    chan_w2_moments,
):
    n_mp = 4
    slots, s_true, c = tokens.shape
    hidden = token_w1.shape[1]
    h = chan_w1.shape[1]
    own = slots // n_mp
    s = -(-s_true // 8) * 8
    pad = s - s_true
    i = lax.axis_index("dp")
    j = lax.axis_index("mp")
    swap_mp = lambda values, bit: swap(values, "mp", n_mp, bit)

    w_own = jnp.concatenate([chan_w1.astype(bf), chan_w2.astype(bf)], axis=0)
    b_own = chan_b1[None]
    b_x = swap_mp(b_own, 2)
    b_core, b_diag = (row[None] for row in swap_mp(jnp.concatenate([b_own, b_x], axis=0), 1))
    w_core = swap_mp(w_own, 1)
    w_x = swap_mp(w_own, 2)
    w_diag = swap_mp(w_x, 1)

    live = jnp.sum(jnp.where(jnp.arange(counts.shape[0]) == i, counts, 0))
    total = jnp.sum(counts).astype(f32)
    slot = j * own + jnp.arange(own)
    row_weight = jnp.where(slot < live, 1.0, 0.0).astype(f32) / total

    def my_images(values):
        mine = lax.dynamic_slice_in_dim(values, j * own, own, 0)
        return jnp.pad(mine, ((0, 0), (0, pad), (0, 0)))

    x = my_images(tokens)
    ct = my_images(cotangent)
    t1 = jnp.pad(token_w1.astype(bf), ((0, pad), (0, 0)))
    t2 = jnp.pad(token_w2.astype(bf), ((0, 0), (0, pad)))
    tb1 = token_bias[:hidden, None]
    tb2 = jnp.pad(token_bias[hidden:], (0, pad))[:, None]

    mixed, second, low, t_act, t_slope = token_fwd(row_weight, x, ct, t1.T, t2.T, tb1, tb2, vec_params)
    flat = lambda a: a.reshape(own * s, c)
    images = lambda a: a.reshape(own, s, c)
    second = flat(second)
    low = flat(low)
    o0, q0, d0, e0 = chan(second, low, w_own, b_own)
    o1, q1, d1, e1 = chan(second, low, w_core, b_core)
    o3, q3, d3, e3 = chan(second, low, w_diag, b_diag)
    o2, q2, d2, e2 = chan(second, low, w_x, b_x)

    out = make_output(mixed, [images(o) for o in (o0, o1, o2, o3)], vec_params)
    out_core = swap_mp(out, 1)
    out_x = swap_mp(out, 2)
    out_diag = swap_mp(out_x, 1)
    order = j.reshape(1).astype(jnp.int32)
    output = gather_images(order, [out, out_core, out_x, out_diag], s_true)

    add = lambda a, b: (a.astype(f32) + b.astype(f32)).astype(bf)
    mine = add(d0, swap_mp(d1, 1))
    theirs = add(d2, swap_mp(d3, 1))
    bits = bits_of(n_dp)
    orders = (bits, bits[1:] + bits[:1])
    sums = []
    for part, order_bits in enumerate(orders):
        a = mine[:c] if part == 0 else mine[c:]
        b = theirs[:c] if part == 0 else theirs[c:]
        for bit in order_bits:
            a = halve(a, "dp", n_dp, bit)
        for bit in order_bits:
            b = halve(b, "dp", n_dp, bit)
        a = add(a, swap_mp(b, 2))
        for bit in order_bits[::-1]:
            a = double(a, "dp", n_dp, bit)
        sums.append(a.astype(f32))
    chan_w1_sum, chan_w2_sum = sums

    ig, grads = token_bwd(
        row_weight, x, ct, mixed, [images(q) for q in (q0, q1, q2, q3)], t_act, t_slope, t1, t2, vec_params
    )
    ig_core = swap_mp(ig, 1)
    ig_x = swap_mp(ig, 2)
    ig_diag = swap_mp(ig_x, 1)
    input_grad = gather_images(order, [ig, ig_core, ig_x, ig_diag], s_true)

    shard_ids = jnp.arange(8)[:, None]
    b1_rows = sum(jnp.where(shard_ids == (j ^ m), e, 0.0) for m, e in enumerate((e0, e1, e2, e3)))
    small = jnp.concatenate([grads, b1_rows], axis=0)
    used = small.shape[0]
    small = jnp.pad(small, ((0, -used % 32), (0, 0))).astype(bf)
    small = halve(small, "mp", n_mp, 1)
    small = halve(small, "mp", n_mp, 2)
    for bit in bits:
        small = add_swapped(small, "dp", n_dp, bit)
    small = double(small, "mp", n_mp, 2)
    small = double(small, "mp", n_mp, 1)
    small = small.astype(f32)
    token_w1_sum = small[:s_true, :hidden]
    token_w2_sum = small[:s_true, hidden : 2 * hidden].T
    vec_sum = small[s : s + 5]
    token_bias_sum = small[s + 5, : hidden + s_true]
    chan_b1_sum = lax.dynamic_slice_in_dim(small, s + 8 + j, 1, 0)[0]

    vec_moments_new = new_moments(vec_moments, vec_sum)
    token_w1_new, token_w1_moments_new = adam_update(token_w1, token_w1_moments, token_w1_sum)
    token_w2_new, token_w2_moments_new = adam_update(token_w2, token_w2_moments, token_w2_sum)
    token_bias_new, token_bias_moments_new = adam_update(token_bias, token_bias_moments, token_bias_sum)
    chan_w1_new, chan_w1_moments_new = adam_update(chan_w1, chan_w1_moments, chan_w1_sum)
    chan_b1_new, chan_b1_moments_new = adam_update(chan_b1, chan_b1_moments, chan_b1_sum)
    chan_w2_new, chan_w2_moments_new = adam_update(chan_w2, chan_w2_moments, chan_w2_sum)
    return (
        output,
        input_grad,
        vec_moments_new,
        token_w1_new,
        token_w1_moments_new,
        token_w2_new,
        token_w2_moments_new,
        token_bias_new,
        token_bias_moments_new,
        chan_w1_new,
        chan_w1_moments_new,
        chan_b1_new,
        chan_b1_moments_new,
        chan_w2_new,
        chan_w2_moments_new,
    )


def solution(mesh):
    placed = (
        P("dp", None, None),
        P("dp", None, None),
        P(),
        P(),
        P(),
        P(),
        P(),
        P(),
        P(),
        P(),
        P(),
        P(None, "mp"),
        P(None, None, "mp"),
        P("mp"),
        P(None, "mp"),
        P("mp", None),
        P(None, "mp", None),
    )
    return jax.shard_map(
        functools.partial(shards, mesh.shape["dp"]),
        mesh=mesh,
        in_specs=placed,
        out_specs=(
            P("dp", None, None),
            P("dp", None, None),
            P(),
            P(),
            P(),
            P(),
            P(),
            P(),
            P(),
            P(None, "mp"),
            P(None, None, "mp"),
            P("mp"),
            P(None, "mp"),
            P("mp", None),
            P(None, "mp", None),
        ),
        check_vma=False,
    )
```

```python
import functools
import jax
import jax.numpy as jnp
from jax import lax
from jax.experimental import pallas as pl
from jax.experimental.pallas import tpu as pltpu
from jax.sharding import PartitionSpec as P

STEP = 4
norm_eps = 1e-06
learn_rate = 0.02
decay_rate = 0.5
weight_decay = 0.05
adam_eps = 1e-08

bf = jnp.bfloat16
f32 = jnp.float32
VMEM_LIMIT = 60 << 20
CHAN_LIMIT = 30 << 20
IG_PIECES = 3
SHORT = pl.CostEstimate(flops=1, transcendentals=0, bytes_accessed=1)


def sds(shape, dtype):
    return jax.ShapeDtypeStruct(shape, dtype)


def dot_nn(a, b):
    return jnp.dot(a, b, preferred_element_type=f32)


def dot_nt(a, b):
    return lax.dot_general(a, b, (((1,), (1,)), ((), ())), preferred_element_type=f32)


def dot_tn(a, b):
    return lax.dot_general(a, b, (((0,), (0,)), ((), ())), preferred_element_type=f32)


def gelu_pair(v):
    cdf = 0.5 * (1.0 + lax.erf(v * 0.7071067811865476))
    pdf = jnp.exp(-0.5 * v * v) * 0.3989422804014327
    return v * cdf, cdf + v * pdf


def norm_parts(values):
    center = values - jnp.mean(values, axis=-1, keepdims=True)
    inv_std = lax.rsqrt(jnp.mean(center * center, axis=-1, keepdims=True) + norm_eps)
    return center * inv_std, inv_std


def row_mean(values):
    return jnp.mean(values, axis=-1, keepdims=True)


def col_sum(values):
    return jnp.sum(values, axis=0, keepdims=True)


def far_from_core(*values):
    return [pltpu.with_memory_space_constraint(v, pltpu.HBM) for v in values]


def token_fwd_kernel(
    rw_ref, x_ref, ct_ref, w1t_ref, w2t_ref, b1_ref, b2_ref, vec_ref,
    mixed_ref, second_ref, low_ref, act_ref, slope_ref,
):
    b = pl.program_id(0)
    x = x_ref[0].astype(f32)
    hat1, _ = norm_parts(x)
    normed = (hat1 * vec_ref[0:1] + vec_ref[1:2]).astype(bf)
    act, slope = gelu_pair(dot_nn(w1t_ref[...], normed) + b1_ref[...])
    act = act.astype(bf)
    act_ref[0] = act
    slope_ref[0] = slope.astype(bf)
    mixed = x + (dot_nn(w2t_ref[...], act) + b2_ref[...])
    mixed_ref[0] = mixed
    hat2, _ = norm_parts(mixed)
    second_ref[0] = (hat2 * vec_ref[2:3] + vec_ref[3:4]).astype(bf)
    low_ref[0] = (ct_ref[0].astype(f32) * rw_ref[b]).astype(bf)


def image_spec(*shape):
    return pl.BlockSpec((1,) + shape, lambda b: (b, 0, 0))


def whole_spec(*shape):
    return pl.BlockSpec(shape, lambda b: (0,) * len(shape))


SMEM_SPEC = pl.BlockSpec(memory_space=pltpu.SMEM)
VMEM_SPEC = pl.BlockSpec(memory_space=pltpu.VMEM)


def token_fwd(rw, x, ct, w1t, w2t, b1, b2, vec):
    n, s, c = x.shape
    k = w1t.shape[0]
    return pl.pallas_call(
        token_fwd_kernel,
        grid=(n,),
        in_specs=[SMEM_SPEC, image_spec(s, c), image_spec(s, c)]
        + [whole_spec(*a.shape) for a in (w1t, w2t, b1, b2, vec)],
        out_specs=[image_spec(s, c)] * 3 + [image_spec(k, c)] * 2,
        out_shape=[pltpu.HBM((n, s, c), f32), pltpu.VMEM((n, s, c), bf), pltpu.VMEM((n, s, c), bf)]
        + [pltpu.HBM((n, k, c), bf)] * 2,
        compiler_params=pltpu.CompilerParams(vmem_limit_bytes=59 << 20),
        cost_estimate=SHORT,
        name="token_fwd",
    )(rw, x, ct, w1t, w2t, b1, b2, vec)


def bias_row(w_ref, c):
    rows = w_ref[2 * c : 2 * c + 8].astype(f32)
    return (rows[0:1] + rows[1:2]) + rows[2:3]


def pack_kernel(w1_ref, w2_ref, b_ref, o_ref):
    c = w1_ref.shape[0]
    o_ref[:c] = w1_ref[...].astype(bf)
    o_ref[c : 2 * c] = w2_ref[...].astype(bf)
    b = b_ref[...]
    hi = b.astype(bf).astype(f32)
    mid = (b - hi).astype(bf).astype(f32)
    low = b - hi - mid
    o_ref[2 * c :] = jnp.concatenate([hi, mid, low, jnp.zeros((5, c), f32)], axis=0).astype(bf)


def pack_weights(w1, w2, b):
    c = w1.shape[0]
    return pl.pallas_call(
        pack_kernel,
        in_specs=[VMEM_SPEC] * 3,
        out_specs=VMEM_SPEC,
        out_shape=sds((2 * c + 8, c), bf),
        compiler_params=pltpu.CompilerParams(vmem_limit_bytes=VMEM_LIMIT),
        cost_estimate=SHORT,
        name="pack_weights",
    )(w1, w2, b)


def take_kernel(s_true, where_ref, x_lo, x_hi, ct_lo, ct_hi, x_ref, ct_ref):
    n, block, c = x_ref.shape
    rows = pl.program_id(0) * block + lax.broadcasted_iota(jnp.int32, (1, block, 1), 1)
    for j in range(4):
        first = j * n
        lo = first // 8 * 8

        @pl.when(where_ref[0] == j)
        def _():
            for lo_ref, hi_ref, o_ref in ((x_lo, x_hi, x_ref), (ct_lo, ct_hi, ct_ref)):
                end = first + n - lo
                mine = lo_ref[:, first - lo : min(end, 8), :]
                if end > 8:
                    mine = jnp.concatenate([mine, hi_ref[:, : end - 8, :]], axis=1)
                mine = jnp.swapaxes(mine, 0, 1)
                o_ref[...] = jnp.where(rows < s_true, mine.astype(f32), 0.0).astype(bf)


def take_images(where, tokens, cotangent, n, s, block=40):
    s_true, _, c = tokens.shape
    lo = pl.BlockSpec((block, 8, c), lambda i, where: (i, (where[0] * n) // 8, 0))
    hi = pl.BlockSpec((block, 8, c), lambda i, where: (i, (where[0] * n + n - 1) // 8, 0))
    mine = pl.BlockSpec((n, block, c), lambda i, where: (0, i, 0))
    return pl.pallas_call(
        functools.partial(take_kernel, s_true),
        grid_spec=pltpu.PrefetchScalarGridSpec(
            num_scalar_prefetch=1, grid=(s // block,), in_specs=[lo, hi, lo, hi], out_specs=[mine, mine]
        ),
        out_shape=[pltpu.HBM((n, s, c), bf)] * 2,
        compiler_params=pltpu.CompilerParams(vmem_limit_bytes=VMEM_LIMIT),
        cost_estimate=SHORT,
        name="take_images",
    )(where, tokens, tokens, cotangent, cotangent)


class Outs:
    def __init__(self, sems):
        self.sems, self.copies = sems, []

    def put(self, value, here, there):
        here[...] = value.astype(bf)
        copy = pltpu.make_async_copy(here, there, self.sems.at[len(self.copies)])
        copy.start()
        self.copies.append(copy)

    def wait(self):
        for copy in self.copies:
            copy.wait()


def chan_fwd_kernel(s_ref, g_ref, w_ref, o_out, dw2_out, slope_ref, o_ref, dw2_ref, sems):
    c = s_ref.shape[1]
    outs = Outs(sems)
    act, slope = gelu_pair(dot_nn(s_ref[...], w_ref[:c]) + bias_row(w_ref, c))
    act = act.astype(bf)
    outs.put(dot_nn(act, w_ref[c : 2 * c]), o_ref, o_out)
    slope_ref[...] = slope.astype(bf)
    outs.put(dot_tn(act, g_ref[...]), dw2_ref, dw2_out)
    outs.wait()


def chan_last_kernel(
    s_ref, g_ref, w_ref, vec_ref, o0, o1, o2, mixed, out_out, dw2_out, slope_ref,
    p0, p1, p2, mixed_ref, out_ref, dw2_ref, in_sems, sems,
):
    c = s_ref.shape[1]
    outs = Outs(sems)
    moves = [
        pltpu.make_async_copy(a, b, in_sems.at[k])
        for k, (a, b) in enumerate(((o0, p0), (o1, p1), (o2, p2), (mixed, mixed_ref)))
    ]
    for move in moves:
        move.start()
    act, slope = gelu_pair(dot_nn(s_ref[...], w_ref[:c]) + bias_row(w_ref, c))
    act = act.astype(bf)
    slope_ref[...] = slope.astype(bf)
    last = dot_nn(act, w_ref[c : 2 * c])
    for move in moves:
        move.wait()
    total = (p0[...].astype(f32) + p1[...].astype(f32)) + (p2[...].astype(f32) + last.astype(bf).astype(f32))
    outs.put(mixed_ref[...] + (total + vec_ref[4:5]), out_ref, out_out)
    outs.put(dot_tn(act, g_ref[...]), dw2_ref, dw2_out)
    outs.wait()


def chan_last(s, g, w, vec, parts, mixed):
    r, c = s.shape
    return pl.pallas_call(
        chan_last_kernel,
        in_specs=[VMEM_SPEC] * 4 + [ANY_SPEC] * 4,
        out_specs=[HBM_SPEC] * 2 + [VMEM_SPEC],
        out_shape=[pltpu.HBM((r, c), bf), pltpu.HBM((c, c), bf), pltpu.VMEM((r, c), bf)],
        scratch_shapes=[pltpu.VMEM((r, c), bf)] * 3
        + [pltpu.VMEM((r, c), f32), pltpu.VMEM((r, c), bf), pltpu.VMEM((c, c), bf)]
        + [pltpu.SemaphoreType.DMA((4,))] * 2,
        compiler_params=pltpu.CompilerParams(vmem_limit_bytes=40 << 20),
        cost_estimate=SHORT,
        name="chan_last",
    )(s, g, w, vec, *far_from_core(*parts, mixed))


def chan_bwd_kernel(s_ref, g_ref, w_ref, slope_ref, q_out, dw1_out, db1_ref, q_ref, dw1_ref, sems):
    c = s_ref.shape[1]
    outs = Outs(sems)
    pre_grad = (dot_nt(g_ref[...], w_ref[c : 2 * c]) * slope_ref[...].astype(f32)).astype(bf)
    db1_ref[...] = col_sum(pre_grad.astype(f32))
    outs.put(dot_nt(pre_grad, w_ref[:c]), q_ref, q_out)
    outs.put(dot_tn(s_ref[...], pre_grad), dw1_ref, dw1_out)
    outs.wait()


def chan_kernel(s_ref, g_ref, w_ref, o_out, q_out, dw_out, db1_ref, o_ref, q_ref, dw_ref, sems):
    c = s_ref.shape[1]
    outs = Outs(sems)
    s = s_ref[...]
    g = g_ref[...]
    w1 = w_ref[:c]
    w2 = w_ref[c : 2 * c]
    act, slope = gelu_pair(dot_nn(s, w1) + bias_row(w_ref, c))
    act = act.astype(bf)
    pre_grad = (dot_nt(g, w2) * slope).astype(bf)
    db1_ref[...] = col_sum(pre_grad.astype(f32))
    outs.put(dot_nn(act, w2), o_ref, o_out)
    outs.put(dot_nt(pre_grad, w1), q_ref, q_out)
    outs.put(dot_tn(act, g), dw_ref.at[1], dw_out.at[1])
    outs.put(dot_tn(s, pre_grad), dw_ref.at[0], dw_out.at[0])
    outs.wait()


HBM_SPEC = pl.BlockSpec(memory_space=pltpu.HBM)
ANY_SPEC = pl.BlockSpec(memory_space=pl.ANY)


def chan_call(kernel, name, operands, large, small):
    return pl.pallas_call(
        kernel,
        in_specs=[VMEM_SPEC] * len(operands),
        out_specs=[HBM_SPEC] * len(large) + [VMEM_SPEC] * len(small),
        out_shape=[pltpu.HBM(shape, bf) for shape in large] + small,
        scratch_shapes=[pltpu.VMEM(shape, bf) for shape in large] + [pltpu.SemaphoreType.DMA((4,))],
        compiler_params=pltpu.CompilerParams(vmem_limit_bytes=CHAN_LIMIT),
        cost_estimate=SHORT,
        name=name,
    )(*operands)


def chan(s, g, w):
    r, c = s.shape
    return chan_call(chan_kernel, "chan", (s, g, w), [(r, c), (r, c), (2, c, c)], [sds((1, c), f32)])


def chan_fwd(s, g, w):
    r, c = s.shape
    return chan_call(chan_fwd_kernel, "chan_fwd", (s, g, w), [(r, c), (c, c)], [pltpu.VMEM((r, c), bf)])


def chan_bwd(s, g, w, slope):
    r, c = s.shape
    return chan_call(chan_bwd_kernel, "chan_bwd", (s, g, w, slope), [(r, c), (c, c)], [sds((1, c), f32)])


def token_bwd_kernel(
    edges, rw_ref, x_ref, ct_ref, mixed_ref, sg0, sg1, sg2, sg3, act_ref, slope_ref, w1_ref, w2_ref, vec_ref, *out_refs
):
    b = pl.program_id(0)
    *ig_refs, grads_ref = out_refs
    s, k = w1_ref.shape
    x = x_ref[0].astype(f32)
    hat1, r1 = norm_parts(x)
    normed = (hat1 * vec_ref[0:1] + vec_ref[1:2]).astype(bf)
    hat2, r2 = norm_parts(mixed_ref[0])
    sg = (sg0[0].astype(f32) + sg1[0].astype(f32)) + (sg2[0].astype(f32) + sg3[0].astype(f32))
    grad_out = ct_ref[0].astype(f32) * rw_ref[b]
    grad_low = grad_out.astype(bf).astype(f32)
    h2 = sg * vec_ref[2:3]
    mixed_grad = grad_out + r2 * (h2 - row_mean(h2) - hat2 * row_mean(h2 * hat2))
    token_grad = mixed_grad.astype(bf)
    pre_grad = (dot_nn(w2_ref[...], token_grad) * slope_ref[0].astype(f32)).astype(bf)
    w1_grad = dot_nt(normed, pre_grad)
    w2_grad = dot_nt(token_grad, act_ref[0])
    normed_grad = dot_nn(w1_ref[...], pre_grad)
    h1 = normed_grad * vec_ref[0:1]
    ig = mixed_grad + r1 * (h1 - row_mean(h1) - hat1 * row_mean(h1 * hat1))
    ig = ig.astype(bf)
    for first, end, ig_ref in zip(edges, edges[1:], ig_refs):

        @pl.when((b >= first) & (b < end))
        def _():
            ig_ref[0] = ig

    ones = jnp.ones((8, x.shape[1]), bf)
    in_row = dot_nt(ones, pre_grad)[0:1]
    out_row = dot_nt(ones, token_grad)[0:1]
    rows = [
        col_sum(normed_grad * hat1), col_sum(normed_grad), col_sum(sg * hat2), col_sum(sg), col_sum(grad_low),
    ]

    @pl.when(b == 0)
    def _():
        grads_ref[...] = jnp.zeros_like(grads_ref)

    grads_ref[0:s, 0:k] += w1_grad
    grads_ref[0:s, k : 2 * k] += w2_grad
    for i, row in enumerate(rows):
        grads_ref[s + i : s + i + 1, :] += row
    grads_ref[s + 5 : s + 6, 0:k] += in_row
    grads_ref[s + 5 : s + 6, k : k + s] += out_row


def piece_spec(first, end, s, c):
    return pl.BlockSpec((1, s, c), lambda b: (jnp.clip(b - first, 0, end - first - 1), 0, 0))


def token_bwd(edges, rw, x, ct, mixed, sgs, act, slope, w1, w2, vec):
    n, s, c = x.shape
    k = w1.shape[1]
    return pl.pallas_call(
        functools.partial(token_bwd_kernel, edges),
        grid=(n,),
        in_specs=[SMEM_SPEC] + [image_spec(s, c)] * 7 + [image_spec(k, c)] * 2
        + [whole_spec(*a.shape) for a in (w1, w2, vec)],
        out_specs=[piece_spec(a, b, s, c) for a, b in zip(edges, edges[1:])] + [whole_spec(s + 8, c)],
        out_shape=[pltpu.HBM((b - a, s, c), bf) for a, b in zip(edges, edges[1:])] + [sds((s + 8, c), f32)],
        compiler_params=pltpu.CompilerParams(vmem_limit_bytes=VMEM_LIMIT),
        cost_estimate=SHORT,
        name="token_bwd",
    )(rw, x, ct, mixed, *sgs, act, slope, w1, w2, vec)


def gather_kernel(counts, order_ref, *refs):
    o_ref = refs[-1]
    groups = []
    at = 0
    for count in counts:
        groups.append(refs[at : at + count])
        at += count
    for j in range(4):

        @pl.when(order_ref[0] == j)
        def _():
            images = [ref[...] for k in range(4) for ref in groups[j ^ k]]
            o_ref[...] = jnp.swapaxes(jnp.concatenate(images, axis=0), 0, 1)


def gather_images(order, own, near, far, diag, s_true, block=40):
    parts = [*own, *near, *far, *diag]
    n = sum(part.shape[0] for part in own)
    _, s, c = own[0].shape
    out = pl.pallas_call(
        functools.partial(gather_kernel, [len(group) for group in (own, near, far, diag)]),
        grid=(s // block,),
        in_specs=[SMEM_SPEC] + [pl.BlockSpec((part.shape[0], block, c), lambda i: (0, i, 0)) for part in parts],
        out_specs=pl.BlockSpec((block, 4 * n, c), lambda i: (i, 0, 0)),
        out_shape=sds((s_true, 4 * n, c), bf),
        compiler_params=pltpu.CompilerParams(vmem_limit_bytes=VMEM_LIMIT),
        cost_estimate=SHORT,
        name="gather_images",
    )(order, *far_from_core(*parts))
    return jnp.swapaxes(out, 0, 1)


def split_add_kernel(upper_ref, a_ref, b_ref, keep_ref, send_ref):
    total = (a_ref[0].astype(f32) + b_ref[0].astype(f32)).astype(bf)

    @pl.when(upper_ref[0] == 0)
    def _():
        keep_ref[0] = total[0]
        send_ref[0] = total[1]

    @pl.when(upper_ref[0] != 0)
    def _():
        keep_ref[0] = total[1]
        send_ref[0] = total[0]


def split_add(upper, a, b):
    n, _, rows, c = a.shape
    whole = pl.BlockSpec((1, 2, rows, c), lambda i: (i, 0, 0, 0))
    half = pl.BlockSpec((1, rows, c), lambda i: (i, 0, 0))
    return pl.pallas_call(
        split_add_kernel,
        grid=(n,),
        in_specs=[SMEM_SPEC, whole, whole],
        out_specs=[half, half],
        out_shape=[sds((n, rows, c), bf)] * 2,
        compiler_params=pltpu.CompilerParams(vmem_limit_bytes=16 << 20),
        cost_estimate=SHORT,
        name="split_add",
    )(upper, *far_from_core(a, b))


def update_kernel(inner, upper_ref, own_ref, got_ref, w_ref, m_ref, w_out, m_out):
    t = pl.program_id(0)
    digit = lax.rem(t, 2) if inner else t // 2
    grads = jnp.where(digit == upper_ref[0], own_ref[...].astype(f32), got_ref[...].astype(f32))
    grads = grads.reshape(w_ref.shape)
    w_new, first, second = adam_parts(w_ref[...], m_ref[0], m_ref[1], grads)
    w_out[...] = w_new
    m_out[0] = first
    m_out[1] = second


def update(inner, upper, own, got, weight, moments):
    rows, c = weight.shape
    block = rows // 4
    own = own.reshape(2, block, c)
    got = got.reshape(2, block, c)
    half = pl.BlockSpec((1, block, c), lambda t: ((t // 2 if inner else lax.rem(t, 2)), 0, 0))
    w_spec = pl.BlockSpec((block, c), lambda t: (t, 0))
    m_spec = pl.BlockSpec((2, block, c), lambda t: (0, t, 0))
    return pl.pallas_call(
        functools.partial(update_kernel, inner),
        grid=(4,),
        in_specs=[SMEM_SPEC, half, half, w_spec, m_spec],
        out_specs=[w_spec, m_spec],
        out_shape=[sds(weight.shape, f32), sds(moments.shape, f32)],
        compiler_params=pltpu.CompilerParams(vmem_limit_bytes=VMEM_LIMIT),
        cost_estimate=SHORT,
        name="update",
    )(upper, own, got, weight, moments)


def swap(values, axis, size, bit):
    return lax.ppermute(values, axis, [(i, i ^ bit) for i in range(size)])


class Box:
    def __init__(self, v):
        self.v = v


class Chain:
    def __init__(self):
        self.last = None

    def tie(self, box):
        if self.last is not None and self.last is not box:
            box.v, self.last.v = lax.optimization_barrier((box.v, self.last.v))
        return box

    def mark(self, box):
        self.last = box
        return box

    def end(self, box):
        return self.mark(self.tie(box))


def add(a, b):
    return (a.astype(f32) + b.astype(f32)).astype(bf)


def upper_of(axis, bit):
    return (lax.axis_index(axis) // bit) % 2


def half_of(values, dim, which):
    return lax.dynamic_index_in_dim(values, which, dim, keepdims=False)


def reduce_steps(chain, box, axis, size, bits):
    for bit in bits:
        upper = upper_of(axis, bit)
        got = Box(swap(half_of(box.v, 0, 1 - upper), axis, size, bit))
        yield
        chain.tie(got)
        box = chain.mark(Box(add(half_of(box.v, 0, upper), got.v)))
    return box


def gather_steps(chain, box, axis, size, bits):
    have = []
    for bit in bits:
        got = Box(swap(box.v, axis, size, bit))
        yield
        chain.tie(got)
        have = sorted(have + [bit])
        dim = have.index(bit)
        box = chain.mark(
            Box(
                jnp.where(
                    upper_of(axis, bit) == 0,
                    jnp.stack([box.v, got.v], axis=dim),
                    jnp.stack([got.v, box.v], axis=dim),
                )
            )
        )
    return box


class Flow:
    def __init__(self, steps):
        self.steps, self.value, self.ended = steps, None, False
        self.go()

    def go(self):
        if self.ended:
            return
        try:
            next(self.steps)
        except StopIteration as stop:
            self.value, self.ended = stop.value, True


def bits_of(size):
    return [1 << b for b in range(size.bit_length() - 1)]


def adam_parts(weight, first, second, grads):
    first = decay_rate * first + (1.0 - decay_rate) * grads
    second = decay_rate * second + (1.0 - decay_rate) * grads * grads
    scale = 1.0 / (1.0 - decay_rate**STEP)
    step_size = first * scale / (jnp.sqrt(second * scale) + adam_eps)
    return weight - learn_rate * (step_size + weight_decay * weight), first, second


def adam_update(weight, moments, grads):
    weight, first, second = adam_parts(weight, moments[0], moments[1], grads)
    return weight, jnp.stack([first, second])


def new_moments(moments, grads):
    first = decay_rate * moments[0] + (1.0 - decay_rate) * grads
    second = decay_rate * moments[1] + (1.0 - decay_rate) * grads * grads
    return jnp.stack([first, second])


def shards(
    n_dp,
    tokens,
    cotangent,
    counts,
    vec_params,
    vec_moments,
    token_w1,
    token_w1_moments,
    token_w2,
    token_w2_moments,
    token_bias,
    token_bias_moments,
    chan_w1,
    chan_w1_moments,
    chan_b1,
    chan_b1_moments,
    chan_w2,
    chan_w2_moments,
):
    n_mp = 4
    slots, s_true, c = tokens.shape
    hidden = token_w1.shape[1]
    h = chan_w1.shape[1]
    own = slots // n_mp
    s = -(-s_true // 8) * 8
    pad = s - s_true
    i = lax.axis_index("dp")
    j = lax.axis_index("mp")
    swap_mp = lambda values, bit: swap(values, "mp", n_mp, bit)

    w_own = pack_weights(chan_w1, chan_w2, chan_b1[None])
    w_x = swap_mp(w_own, 2)
    w_core = swap_mp(w_own, 1)

    live = jnp.sum(jnp.where(jnp.arange(counts.shape[0]) == i, counts, 0))
    total = jnp.sum(counts).astype(f32)
    slot = j * own + jnp.arange(own)
    row_weight = jnp.where(slot < live, 1.0, 0.0).astype(f32) / total

    order = j.reshape(1).astype(jnp.int32)
    x, ct = take_images(order, jnp.swapaxes(tokens, 0, 1), jnp.swapaxes(cotangent, 0, 1), own, s)
    t1 = jnp.pad(token_w1.astype(bf), ((0, pad), (0, 0)))
    t2 = jnp.pad(token_w2.astype(bf), ((0, 0), (0, pad)))
    tb1 = token_bias[:hidden, None]
    tb2 = jnp.pad(token_bias[hidden:], (0, pad))[:, None]

    chain = Chain()
    digits = bits_of(n_dp)
    halved, exchanged = digits[:2], digits[2:]
    flat = lambda a: a.reshape(own * s, c)
    images = lambda a: a.reshape(own, s, c)
    upper = {bit: upper_of("dp", bit).reshape(1).astype(jnp.int32) for bit in digits}
    swap_dp = lambda values, bit: swap(values, "dp", n_dp, bit)

    def sum_steps(a, b, bits):
        parts = a.v.shape[0]
        left = list(halved)
        for bit in bits:
            at = left.index(bit)
            rows = a.v.shape[0] * a.v.shape[1] // (2 ** (at + 1) * parts)
            view = lambda v: v.reshape(-1, 2, rows, c)
            chain.tie(b)
            keep, send = split_add(upper[bit], view(a.v), view(b.v))
            left.remove(bit)
            a = chain.mark(Box(keep))
            b = Box(swap_dp(send, bit))
            yield
        chain.tie(b)
        return chain.mark(Box(add(a.v, b.v).reshape(parts, -1, c)))

    def image_steps(parts):
        far = [Box(swap_mp(part.v, 2)) for part in parts]
        near, diag = [], []
        for at, piece in enumerate(far):
            yield
            chain.end(piece)
            diag.append(Box(swap_mp(piece.v, 1)))
            chain.tie(parts[at])
            near.append(Box(swap_mp(parts[at].v, 1)))
        yield
        for piece in near + diag:
            chain.end(piece)
        yield
        chain.tie(parts[0])
        groups = [[box.v for box in boxes] for boxes in (parts, near, far, diag)]
        return chain.mark(Box(gather_images(order, *groups, s_true)))

    mixed, second, low, t_act, t_slope = token_fwd(row_weight, x, ct, t1.T, t2.T, tb1, tb2, vec_params)
    second = flat(second)
    low = flat(low)
    w_core = Box(w_core)
    w_x = Box(w_x)
    o0, q0, d0, e0 = (Box(v) for v in chan(second, low, w_own))
    chain.mark(o0)
    chain.tie(w_core)
    o1, q1, d1, e1 = (Box(v) for v in chan(second, low, w_core.v))
    chain.mark(o1)
    d1 = Box(swap_mp(d1.v, 1))
    chain.end(w_x)
    w_diag = Box(swap_mp(w_x.v, 1))
    o2, d2b, slope2 = (Box(v) for v in chan_fwd(second, low, w_x.v))
    chain.mark(o2)
    mine = Flow(sum_steps(d0, d1, halved))
    chain.tie(w_diag)
    out, d3b, slope3 = chan_last(second, low, w_diag.v, vec_params, [o0.v, o1.v, o2.v], flat(mixed))
    d3b = Box(swap_mp(d3b, 1))
    slope3 = Box(slope3)
    out = chain.mark(Box(images(out)))
    out = Flow(image_steps([out]))
    chain.tie(slope3)
    q3, d3a, e3 = (Box(v) for v in chan_bwd(second, low, w_diag.v, slope3.v))
    chain.mark(q3)
    mine.go()

    def theirs_steps(part, near, far, bits):
        theirs = yield from sum_steps(near, far, bits)
        got = Box(swap_mp(theirs.v, 2))
        yield
        while not mine.ended:
            mine.go()
        chain.tie(got)
        piece = chain.mark(Box(add(mine.value.v[part], got.v[0])))
        for bit in exchanged:
            got = Box(swap_dp(piece.v, bit))
            yield
            chain.tie(got)
            piece = chain.mark(Box(add(piece.v, got.v)))
        piece = yield from gather_steps(chain, piece, "dp", n_dp, bits[:0:-1])
        got = Box(swap_dp(piece.v, bits[0]))
        yield
        chain.tie(got)
        weight, moments = ((chan_w1, chan_w1_moments), (chan_w2, chan_w2_moments))[part]
        new, moments = (Box(v) for v in update(part == 1, upper[bits[0]], piece.v, got.v, weight, moments))
        chain.mark(new)
        return new, moments

    lead = lambda box: Box(box.v[None])
    theirs2 = Flow(theirs_steps(1, lead(d2b), lead(d3b), halved[::-1]))
    d3a = Box(swap_mp(d3a.v, 1))
    chain.tie(slope2)
    q2, d2a, e2 = (Box(v) for v in chan_bwd(second, low, w_x.v, slope2.v))
    chain.mark(q2)
    theirs1 = Flow(theirs_steps(0, lead(d2a), lead(d3a), halved))
    mine.go()
    chain.tie(q0)
    grads_of = [images(q.v) for q in (q0, q1, q2, q3)]
    edges = [n * own // IG_PIECES for n in range(IG_PIECES + 1)]
    *ig, grads = token_bwd(edges, row_weight, x, ct, mixed, grads_of, t_act, t_slope, t1, t2, vec_params)
    ig = [Box(v) for v in ig]
    chain.mark(ig[0])

    shard_ids = jnp.arange(8)[:, None]
    b1_rows = sum(jnp.where(shard_ids == (j ^ m), e.v, 0.0) for m, e in enumerate((e0, e1, e2, e3)))
    small = jnp.concatenate([grads, b1_rows], axis=0)
    small = jnp.pad(small, ((0, -small.shape[0] % 32), (0, 0))).astype(bf)

    def small_steps(small):
        rows = small.shape[0]
        box = Box(small.reshape(2, rows // 2, c))
        box = yield from reduce_steps(chain, box, "mp", n_mp, [1])
        for axis, size, bit in [("dp", n_dp, bit) for bit in digits] + [("mp", n_mp, 2)]:
            got = Box(swap(box.v, axis, size, bit))
            yield
            chain.tie(got)
            box = chain.mark(Box(add(box.v, got.v)))
        box = yield from gather_steps(chain, box, "mp", n_mp, [1])
        return box.v.reshape(rows, c).astype(f32)

    ig = Flow(image_steps(ig))
    for flow in (theirs2, theirs1, out, out, theirs2, theirs1):
        flow.go()
    small = Flow(small_steps(small))
    for flow in (out, ig, theirs2, theirs1, small, ig, theirs2, theirs1, small, ig, theirs2, theirs1, small, ig, ig):
        flow.go()
    flows = [theirs2, theirs1, small]
    for turn in range(3 * len(digits) + 9):
        for flow in flows:
            flow.go()
    output = out.value.v
    input_grad = ig.value.v
    chan_w1_new, chan_w1_moments_new = (box.v for box in theirs1.value)
    chan_w2_new, chan_w2_moments_new = (box.v for box in theirs2.value)

    small = small.value
    token_w1_sum = small[:s_true, :hidden]
    token_w2_sum = small[:s_true, hidden : 2 * hidden].T
    vec_sum = small[s : s + 5]
    token_bias_sum = small[s + 5, : hidden + s_true]
    chan_b1_sum = lax.dynamic_slice_in_dim(small, s + 8 + j, 1, 0)[0]
    vec_moments_new = new_moments(vec_moments, vec_sum)
    token_w1_new, token_w1_moments_new = adam_update(token_w1, token_w1_moments, token_w1_sum)
    token_w2_new, token_w2_moments_new = adam_update(token_w2, token_w2_moments, token_w2_sum)
    token_bias_new, token_bias_moments_new = adam_update(token_bias, token_bias_moments, token_bias_sum)
    chan_b1_new, chan_b1_moments_new = adam_update(chan_b1, chan_b1_moments, chan_b1_sum)
    return (
        output,
        input_grad,
        vec_moments_new,
        token_w1_new,
        token_w1_moments_new,
        token_w2_new,
        token_w2_moments_new,
        token_bias_new,
        token_bias_moments_new,
        chan_w1_new,
        chan_w1_moments_new,
        chan_b1_new,
        chan_b1_moments_new,
        chan_w2_new,
        chan_w2_moments_new,
    )


def solution(mesh):
    placed = (
        P("dp", None, None),
        P("dp", None, None),
        P(),
        P(),
        P(),
        P(),
        P(),
        P(),
        P(),
        P(),
        P(),
        P(None, "mp"),
        P(None, None, "mp"),
        P("mp"),
        P(None, "mp"),
        P("mp", None),
        P(None, "mp", None),
    )
    return jax.shard_map(
        functools.partial(shards, mesh.shape["dp"]),
        mesh=mesh,
        in_specs=placed,
        out_specs=(
            P("dp", None, None),
            P("dp", None, None),
            P(),
            P(),
            P(),
            P(),
            P(),
            P(),
            P(),
            P(None, "mp"),
            P(None, None, "mp"),
            P("mp"),
            P(None, "mp"),
            P("mp", None),
            P(None, "mp", None),
        ),
        check_vma=False,
    )
```

```python
import functools
import jax
import jax.numpy as jnp
from jax import lax
from jax.experimental import pallas as pl
from jax.experimental.pallas import tpu as pltpu
from jax.sharding import PartitionSpec as P

STEP = 4
norm_eps = 1e-06
learn_rate = 0.02
decay_rate = 0.5
weight_decay = 0.05
adam_eps = 1e-08

bf = jnp.bfloat16
f32 = jnp.float32
VMEM_LIMIT = 60 << 20
CHAN_LIMIT = 30 << 20
SHORT = pl.CostEstimate(flops=1, transcendentals=0, bytes_accessed=1)


def sds(shape, dtype):
    return jax.ShapeDtypeStruct(shape, dtype)


def dot_nn(a, b):
    return jnp.dot(a, b, preferred_element_type=f32)


def dot_nt(a, b):
    return lax.dot_general(a, b, (((1,), (1,)), ((), ())), preferred_element_type=f32)


def dot_tn(a, b):
    return lax.dot_general(a, b, (((0,), (0,)), ((), ())), preferred_element_type=f32)


def gelu_pair(v):
    cdf = 0.5 * (1.0 + lax.erf(v * 0.7071067811865476))
    pdf = jnp.exp(-0.5 * v * v) * 0.3989422804014327
    return v * cdf, cdf + v * pdf


def norm_parts(values):
    center = values - jnp.mean(values, axis=-1, keepdims=True)
    inv_std = lax.rsqrt(jnp.mean(center * center, axis=-1, keepdims=True) + norm_eps)
    return center * inv_std, inv_std


def row_mean(values):
    return jnp.mean(values, axis=-1, keepdims=True)


def col_sum(values):
    return jnp.sum(values, axis=0, keepdims=True)


def far_from_core(*values):
    return [pltpu.with_memory_space_constraint(v, pltpu.HBM) for v in values]


def token_fwd_kernel(
    rw_ref, x_ref, ct_ref, w1t_ref, w2t_ref, b1_ref, b2_ref, vec_ref,
    mixed_ref, second_ref, low_ref, act_ref, slope_ref,
):
    b = pl.program_id(0)
    x = x_ref[0].astype(f32)
    hat1, _ = norm_parts(x)
    normed = (hat1 * vec_ref[0:1] + vec_ref[1:2]).astype(bf)
    act, slope = gelu_pair(dot_nn(w1t_ref[...], normed) + b1_ref[...])
    act = act.astype(bf)
    act_ref[0] = act
    slope_ref[0] = slope.astype(bf)
    mixed = x + (dot_nn(w2t_ref[...], act) + b2_ref[...])
    mixed_ref[0] = mixed
    hat2, _ = norm_parts(mixed)
    second_ref[0] = (hat2 * vec_ref[2:3] + vec_ref[3:4]).astype(bf)
    low_ref[0] = (ct_ref[0].astype(f32) * rw_ref[b]).astype(bf)


def image_spec(*shape):
    return pl.BlockSpec((1,) + shape, lambda b: (b, 0, 0))


def whole_spec(*shape):
    return pl.BlockSpec(shape, lambda b: (0,) * len(shape))


SMEM_SPEC = pl.BlockSpec(memory_space=pltpu.SMEM)
VMEM_SPEC = pl.BlockSpec(memory_space=pltpu.VMEM)


def token_fwd(rw, x, ct, w1t, w2t, b1, b2, vec):
    n, s, c = x.shape
    k = w1t.shape[0]
    return pl.pallas_call(
        token_fwd_kernel,
        grid=(n,),
        in_specs=[SMEM_SPEC, image_spec(s, c), image_spec(s, c)]
        + [whole_spec(*a.shape) for a in (w1t, w2t, b1, b2, vec)],
        out_specs=[image_spec(s, c)] * 3 + [image_spec(k, c)] * 2,
        out_shape=[pltpu.HBM((n, s, c), f32), pltpu.VMEM((n, s, c), bf), pltpu.VMEM((n, s, c), bf)]
        + [pltpu.HBM((n, k, c), bf)] * 2,
        compiler_params=pltpu.CompilerParams(vmem_limit_bytes=59 << 20),
        cost_estimate=SHORT,
        name="token_fwd",
    )(rw, x, ct, w1t, w2t, b1, b2, vec)


def bias_row(w_ref, c):
    rows = w_ref[2 * c : 2 * c + 8].astype(f32)
    return (rows[0:1] + rows[1:2]) + rows[2:3]


def pack_kernel(w1_ref, w2_ref, b_ref, o_ref):
    c = w1_ref.shape[0]
    o_ref[:c] = w1_ref[...].astype(bf)
    o_ref[c : 2 * c] = w2_ref[...].astype(bf)
    b = b_ref[...]
    hi = b.astype(bf).astype(f32)
    mid = (b - hi).astype(bf).astype(f32)
    low = b - hi - mid
    o_ref[2 * c :] = jnp.concatenate([hi, mid, low, jnp.zeros((5, c), f32)], axis=0).astype(bf)


def pack_weights(w1, w2, b):
    c = w1.shape[0]
    return pl.pallas_call(
        pack_kernel,
        in_specs=[VMEM_SPEC] * 3,
        out_specs=VMEM_SPEC,
        out_shape=sds((2 * c + 8, c), bf),
        compiler_params=pltpu.CompilerParams(vmem_limit_bytes=VMEM_LIMIT),
        cost_estimate=SHORT,
        name="pack_weights",
    )(w1, w2, b)


def take_kernel(s_true, where_ref, x_lo, x_hi, ct_lo, ct_hi, x_ref, ct_ref):
    n, block, c = x_ref.shape
    rows = pl.program_id(0) * block + lax.broadcasted_iota(jnp.int32, (1, block, 1), 1)
    for j in range(4):
        first = j * n
        lo = first // 8 * 8

        @pl.when(where_ref[0] == j)
        def _():
            for lo_ref, hi_ref, o_ref in ((x_lo, x_hi, x_ref), (ct_lo, ct_hi, ct_ref)):
                end = first + n - lo
                mine = lo_ref[:, first - lo : min(end, 8), :]
                if end > 8:
                    mine = jnp.concatenate([mine, hi_ref[:, : end - 8, :]], axis=1)
                mine = jnp.swapaxes(mine, 0, 1)
                o_ref[...] = jnp.where(rows < s_true, mine.astype(f32), 0.0).astype(bf)


def take_images(where, tokens, cotangent, n, s, block=40):
    s_true, _, c = tokens.shape
    lo = pl.BlockSpec((block, 8, c), lambda i, where: (i, (where[0] * n) // 8, 0))
    hi = pl.BlockSpec((block, 8, c), lambda i, where: (i, (where[0] * n + n - 1) // 8, 0))
    mine = pl.BlockSpec((n, block, c), lambda i, where: (0, i, 0))
    return pl.pallas_call(
        functools.partial(take_kernel, s_true),
        grid_spec=pltpu.PrefetchScalarGridSpec(
            num_scalar_prefetch=1, grid=(s // block,), in_specs=[lo, hi, lo, hi], out_specs=[mine, mine]
        ),
        out_shape=[pltpu.HBM((n, s, c), bf)] * 2,
        compiler_params=pltpu.CompilerParams(vmem_limit_bytes=VMEM_LIMIT),
        cost_estimate=SHORT,
        name="take_images",
    )(where, tokens, tokens, cotangent, cotangent)


class Outs:
    def __init__(self, sems):
        self.sems, self.copies = sems, []

    def put(self, value, here, there):
        here[...] = value.astype(bf)
        copy = pltpu.make_async_copy(here, there, self.sems.at[len(self.copies)])
        copy.start()
        self.copies.append(copy)

    def wait(self):
        for copy in self.copies:
            copy.wait()


def chan_fwd_kernel(s_ref, g_ref, w_ref, o_out, dw2_out, slope_ref, o_ref, dw2_ref, sems):
    c = s_ref.shape[1]
    outs = Outs(sems)
    act, slope = gelu_pair(dot_nn(s_ref[...], w_ref[:c]) + bias_row(w_ref, c))
    act = act.astype(bf)
    outs.put(dot_nn(act, w_ref[c : 2 * c]), o_ref, o_out)
    slope_ref[...] = slope.astype(bf)
    outs.put(dot_tn(act, g_ref[...]), dw2_ref, dw2_out)
    outs.wait()


def chan_last_kernel(
    s_ref, g_ref, w_ref, vec_ref, o0, o1, o2, mixed, out_out, dw2_out, slope_ref,
    p0, p1, p2, mixed_ref, out_ref, dw2_ref, in_sems, sems,
):
    c = s_ref.shape[1]
    outs = Outs(sems)
    moves = [
        pltpu.make_async_copy(a, b, in_sems.at[k])
        for k, (a, b) in enumerate(((o0, p0), (o1, p1), (o2, p2), (mixed, mixed_ref)))
    ]
    for move in moves:
        move.start()
    act, slope = gelu_pair(dot_nn(s_ref[...], w_ref[:c]) + bias_row(w_ref, c))
    act = act.astype(bf)
    slope_ref[...] = slope.astype(bf)
    last = dot_nn(act, w_ref[c : 2 * c])
    for move in moves:
        move.wait()
    total = (p0[...].astype(f32) + p1[...].astype(f32)) + (p2[...].astype(f32) + last.astype(bf).astype(f32))
    outs.put(mixed_ref[...] + (total + vec_ref[4:5]), out_ref, out_out)
    outs.put(dot_tn(act, g_ref[...]), dw2_ref, dw2_out)
    outs.wait()


def chan_last(s, g, w, vec, parts, mixed):
    r, c = s.shape
    return pl.pallas_call(
        chan_last_kernel,
        in_specs=[VMEM_SPEC] * 4 + [ANY_SPEC] * 4,
        out_specs=[HBM_SPEC] * 2 + [VMEM_SPEC],
        out_shape=[pltpu.HBM((r, c), bf), pltpu.HBM((c, c), bf), pltpu.VMEM((r, c), bf)],
        scratch_shapes=[pltpu.VMEM((r, c), bf)] * 3
        + [pltpu.VMEM((r, c), f32), pltpu.VMEM((r, c), bf), pltpu.VMEM((c, c), bf)]
        + [pltpu.SemaphoreType.DMA((4,))] * 2,
        compiler_params=pltpu.CompilerParams(vmem_limit_bytes=40 << 20),
        cost_estimate=SHORT,
        name="chan_last",
    )(s, g, w, vec, *far_from_core(*parts, mixed))


def chan_bwd_kernel(s_ref, g_ref, w_ref, slope_ref, q_out, dw1_out, db1_ref, q_ref, dw1_ref, sems):
    c = s_ref.shape[1]
    outs = Outs(sems)
    pre_grad = (dot_nt(g_ref[...], w_ref[c : 2 * c]) * slope_ref[...].astype(f32)).astype(bf)
    db1_ref[...] = col_sum(pre_grad.astype(f32))
    outs.put(dot_nt(pre_grad, w_ref[:c]), q_ref, q_out)
    outs.put(dot_tn(s_ref[...], pre_grad), dw1_ref, dw1_out)
    outs.wait()


def chan_kernel(s_ref, g_ref, w_ref, o_out, q_out, dw_out, db1_ref, o_ref, q_ref, dw_ref, sems):
    c = s_ref.shape[1]
    outs = Outs(sems)
    s = s_ref[...]
    g = g_ref[...]
    w1 = w_ref[:c]
    w2 = w_ref[c : 2 * c]
    act, slope = gelu_pair(dot_nn(s, w1) + bias_row(w_ref, c))
    act = act.astype(bf)
    pre_grad = (dot_nt(g, w2) * slope).astype(bf)
    db1_ref[...] = col_sum(pre_grad.astype(f32))
    outs.put(dot_nn(act, w2), o_ref, o_out)
    outs.put(dot_nt(pre_grad, w1), q_ref, q_out)
    outs.put(dot_tn(act, g), dw_ref.at[1], dw_out.at[1])
    outs.put(dot_tn(s, pre_grad), dw_ref.at[0], dw_out.at[0])
    outs.wait()


HBM_SPEC = pl.BlockSpec(memory_space=pltpu.HBM)
ANY_SPEC = pl.BlockSpec(memory_space=pl.ANY)


def chan_call(kernel, name, operands, large, small):
    return pl.pallas_call(
        kernel,
        in_specs=[VMEM_SPEC] * len(operands),
        out_specs=[HBM_SPEC] * len(large) + [VMEM_SPEC] * len(small),
        out_shape=[pltpu.HBM(shape, bf) for shape in large] + small,
        scratch_shapes=[pltpu.VMEM(shape, bf) for shape in large] + [pltpu.SemaphoreType.DMA((4,))],
        compiler_params=pltpu.CompilerParams(vmem_limit_bytes=CHAN_LIMIT),
        cost_estimate=SHORT,
        name=name,
    )(*operands)


def chan(s, g, w):
    r, c = s.shape
    return chan_call(chan_kernel, "chan", (s, g, w), [(r, c), (r, c), (2, c, c)], [sds((1, c), f32)])


def chan_fwd(s, g, w):
    r, c = s.shape
    return chan_call(chan_fwd_kernel, "chan_fwd", (s, g, w), [(r, c), (c, c)], [pltpu.VMEM((r, c), bf)])


def chan_bwd(s, g, w, slope):
    r, c = s.shape
    return chan_call(chan_bwd_kernel, "chan_bwd", (s, g, w, slope), [(r, c), (c, c)], [sds((1, c), f32)])


def token_bwd_kernel(
    rw_ref, x_ref, ct_ref, mixed_ref, sg0, sg1, sg2, sg3, act_ref, slope_ref, w1_ref, w2_ref, vec_ref,
    ig_ref, grads_ref,
):
    b = pl.program_id(0)
    s, k = w1_ref.shape
    x = x_ref[0].astype(f32)
    hat1, r1 = norm_parts(x)
    normed = (hat1 * vec_ref[0:1] + vec_ref[1:2]).astype(bf)
    hat2, r2 = norm_parts(mixed_ref[0])
    sg = (sg0[0].astype(f32) + sg1[0].astype(f32)) + (sg2[0].astype(f32) + sg3[0].astype(f32))
    grad_out = ct_ref[0].astype(f32) * rw_ref[b]
    grad_low = grad_out.astype(bf).astype(f32)
    h2 = sg * vec_ref[2:3]
    mixed_grad = grad_out + r2 * (h2 - row_mean(h2) - hat2 * row_mean(h2 * hat2))
    token_grad = mixed_grad.astype(bf)
    pre_grad = (dot_nn(w2_ref[...], token_grad) * slope_ref[0].astype(f32)).astype(bf)
    w1_grad = dot_nt(normed, pre_grad)
    w2_grad = dot_nt(token_grad, act_ref[0])
    normed_grad = dot_nn(w1_ref[...], pre_grad)
    h1 = normed_grad * vec_ref[0:1]
    ig = mixed_grad + r1 * (h1 - row_mean(h1) - hat1 * row_mean(h1 * hat1))
    ig_ref[0] = ig.astype(bf)
    ones = jnp.ones((8, x.shape[1]), bf)
    in_row = dot_nt(ones, pre_grad)[0:1]
    out_row = dot_nt(ones, token_grad)[0:1]
    rows = [
        col_sum(normed_grad * hat1), col_sum(normed_grad), col_sum(sg * hat2), col_sum(sg), col_sum(grad_low),
    ]

    @pl.when(b == 0)
    def _():
        grads_ref[...] = jnp.zeros_like(grads_ref)

    grads_ref[0:s, 0:k] += w1_grad
    grads_ref[0:s, k : 2 * k] += w2_grad
    for i, row in enumerate(rows):
        grads_ref[s + i : s + i + 1, :] += row
    grads_ref[s + 5 : s + 6, 0:k] += in_row
    grads_ref[s + 5 : s + 6, k : k + s] += out_row


def token_bwd(rw, x, ct, mixed, sgs, act, slope, w1, w2, vec):
    n, s, c = x.shape
    k = w1.shape[1]
    return pl.pallas_call(
        token_bwd_kernel,
        grid=(n,),
        in_specs=[SMEM_SPEC] + [image_spec(s, c)] * 7 + [image_spec(k, c)] * 2
        + [whole_spec(*a.shape) for a in (w1, w2, vec)],
        out_specs=[image_spec(s, c), whole_spec(s + 8, c)],
        out_shape=[pltpu.HBM((n, s, c), bf), sds((s + 8, c), f32)],
        compiler_params=pltpu.CompilerParams(vmem_limit_bytes=VMEM_LIMIT),
        cost_estimate=SHORT,
        name="token_bwd",
    )(rw, x, ct, mixed, *sgs, act, slope, w1, w2, vec)


def gather_kernel(order_ref, *refs):
    o_ref = refs[-1]
    for j in range(4):

        @pl.when(order_ref[0] == j)
        def _():
            images = jnp.concatenate([refs[j ^ k][...] for k in range(4)], axis=0)
            o_ref[...] = jnp.swapaxes(images, 0, 1)


def gather_images(order, parts, s_true, block=40):
    n, s, c = parts[0].shape
    out = pl.pallas_call(
        gather_kernel,
        grid=(s // block,),
        in_specs=[SMEM_SPEC] + [pl.BlockSpec((n, block, c), lambda i: (0, i, 0))] * 4,
        out_specs=pl.BlockSpec((block, 4 * n, c), lambda i: (i, 0, 0)),
        out_shape=sds((s_true, 4 * n, c), bf),
        compiler_params=pltpu.CompilerParams(vmem_limit_bytes=VMEM_LIMIT),
        cost_estimate=SHORT,
        name="gather_images",
    )(order, *far_from_core(*parts))
    return jnp.swapaxes(out, 0, 1)


def split_add_kernel(upper_ref, a_ref, b_ref, keep_ref, send_ref):
    total = (a_ref[0].astype(f32) + b_ref[0].astype(f32)).astype(bf)

    @pl.when(upper_ref[0] == 0)
    def _():
        keep_ref[0] = total[0]
        send_ref[0] = total[1]

    @pl.when(upper_ref[0] != 0)
    def _():
        keep_ref[0] = total[1]
        send_ref[0] = total[0]


def split_add(upper, a, b):
    n, _, rows, c = a.shape
    whole = pl.BlockSpec((1, 2, rows, c), lambda i: (i, 0, 0, 0))
    half = pl.BlockSpec((1, rows, c), lambda i: (i, 0, 0))
    return pl.pallas_call(
        split_add_kernel,
        grid=(n,),
        in_specs=[SMEM_SPEC, whole, whole],
        out_specs=[half, half],
        out_shape=[sds((n, rows, c), bf)] * 2,
        compiler_params=pltpu.CompilerParams(vmem_limit_bytes=16 << 20),
        cost_estimate=SHORT,
        name="split_add",
    )(upper, *far_from_core(a, b))


def update_kernel(inner, upper_ref, own_ref, got_ref, w_in, m_in, w_out, m_out, w_new, m_new, in_sems, out_sems):
    block = w_new.shape[0] // 4

    def pairs(quarter, sems, inwards):
        rows = pl.ds(pl.multiple_of(quarter * block, block), block)
        views = [(w_new.at[rows], (w_in if inwards else w_out).at[rows])]
        views += [(m_new.at[k, rows], (m_in if inwards else m_out).at[k, rows]) for k in range(2)]
        for k, (here, there) in enumerate(views):
            ends = (there, here) if inwards else (here, there)
            yield pltpu.make_async_copy(*ends, sems.at[quarter, k])

    for quarter in range(4):
        for copy in pairs(quarter, in_sems, True):
            copy.start()

    @pl.loop(0, 4)
    def _(quarter):
        for copy in pairs(quarter, in_sems, True):
            copy.wait()
        high, low = quarter // 2, lax.rem(quarter, 2)
        digit, sub = (low, high) if inner else (high, low)
        rows = pl.ds(pl.multiple_of(quarter * block, block), block)
        grads = jnp.where(digit == upper_ref[0], own_ref[sub].astype(f32), got_ref[sub].astype(f32))
        w_new[rows], m_new[0, rows], m_new[1, rows] = adam_parts(w_new[rows], m_new[0, rows], m_new[1, rows], grads)
        for copy in pairs(quarter, out_sems, False):
            copy.start()

    @pl.loop(0, 4)
    def _(quarter):
        for copy in pairs(quarter, out_sems, False):
            copy.wait()


def update(inner, upper, own, got, weight, moments):
    rows, c = weight.shape
    return pl.pallas_call(
        functools.partial(update_kernel, inner),
        in_specs=[SMEM_SPEC] + [VMEM_SPEC] * 2 + [ANY_SPEC] * 2,
        out_specs=[HBM_SPEC] * 2,
        out_shape=[pltpu.HBM(weight.shape, f32), pltpu.HBM(moments.shape, f32)],
        scratch_shapes=[pltpu.VMEM(weight.shape, f32), pltpu.VMEM(moments.shape, f32)]
        + [pltpu.SemaphoreType.DMA((4, 3))] * 2,
        compiler_params=pltpu.CompilerParams(vmem_limit_bytes=20 << 20),
        cost_estimate=SHORT,
        name="update",
    )(upper, own.reshape(2, rows // 4, c), got.reshape(2, rows // 4, c), *far_from_core(weight, moments))


def swap(values, axis, size, bit):
    return lax.ppermute(values, axis, [(i, i ^ bit) for i in range(size)])


class Box:
    def __init__(self, v):
        self.v = v


class Chain:
    def __init__(self):
        self.last = None

    def tie(self, box):
        if self.last is not None and self.last is not box:
            box.v, self.last.v = lax.optimization_barrier((box.v, self.last.v))
        return box

    def mark(self, box):
        self.last = box
        return box

    def end(self, box):
        return self.mark(self.tie(box))


def add(a, b):
    return (a.astype(f32) + b.astype(f32)).astype(bf)


def upper_of(axis, bit):
    return (lax.axis_index(axis) // bit) % 2


def half_of(values, dim, which):
    return lax.dynamic_index_in_dim(values, which, dim, keepdims=False)


def reduce_steps(chain, box, axis, size, bits):
    for bit in bits:
        upper = upper_of(axis, bit)
        got = Box(swap(half_of(box.v, 0, 1 - upper), axis, size, bit))
        yield
        chain.tie(got)
        box = chain.mark(Box(add(half_of(box.v, 0, upper), got.v)))
    return box


def gather_steps(chain, box, axis, size, bits):
    have = []
    for bit in bits:
        got = Box(swap(box.v, axis, size, bit))
        yield
        chain.tie(got)
        have = sorted(have + [bit])
        dim = have.index(bit)
        box = chain.mark(
            Box(
                jnp.where(
                    upper_of(axis, bit) == 0,
                    jnp.stack([box.v, got.v], axis=dim),
                    jnp.stack([got.v, box.v], axis=dim),
                )
            )
        )
    return box


class Flow:
    def __init__(self, steps):
        self.steps, self.value, self.ended = steps, None, False
        self.go()

    def go(self):
        if self.ended:
            return
        try:
            next(self.steps)
        except StopIteration as stop:
            self.value, self.ended = stop.value, True


def bits_of(size):
    return [1 << b for b in range(size.bit_length() - 1)]


def adam_parts(weight, first, second, grads):
    first = decay_rate * first + (1.0 - decay_rate) * grads
    second = decay_rate * second + (1.0 - decay_rate) * grads * grads
    scale = 1.0 / (1.0 - decay_rate**STEP)
    step_size = first * scale / (jnp.sqrt(second * scale) + adam_eps)
    return weight - learn_rate * (step_size + weight_decay * weight), first, second


def adam_update(weight, moments, grads):
    weight, first, second = adam_parts(weight, moments[0], moments[1], grads)
    return weight, jnp.stack([first, second])


def new_moments(moments, grads):
    first = decay_rate * moments[0] + (1.0 - decay_rate) * grads
    second = decay_rate * moments[1] + (1.0 - decay_rate) * grads * grads
    return jnp.stack([first, second])


def shards(
    n_dp,
    tokens,
    cotangent,
    counts,
    vec_params,
    vec_moments,
    token_w1,
    token_w1_moments,
    token_w2,
    token_w2_moments,
    token_bias,
    token_bias_moments,
    chan_w1,
    chan_w1_moments,
    chan_b1,
    chan_b1_moments,
    chan_w2,
    chan_w2_moments,
):
    n_mp = 4
    slots, s_true, c = tokens.shape
    hidden = token_w1.shape[1]
    h = chan_w1.shape[1]
    own = slots // n_mp
    s = -(-s_true // 8) * 8
    pad = s - s_true
    i = lax.axis_index("dp")
    j = lax.axis_index("mp")
    swap_mp = lambda values, bit: swap(values, "mp", n_mp, bit)

    w_own = pack_weights(chan_w1, chan_w2, chan_b1[None])
    w_x = swap_mp(w_own, 2)
    w_core = swap_mp(w_own, 1)

    live = jnp.sum(jnp.where(jnp.arange(counts.shape[0]) == i, counts, 0))
    total = jnp.sum(counts).astype(f32)
    slot = j * own + jnp.arange(own)
    row_weight = jnp.where(slot < live, 1.0, 0.0).astype(f32) / total

    order = j.reshape(1).astype(jnp.int32)
    x, ct = take_images(order, jnp.swapaxes(tokens, 0, 1), jnp.swapaxes(cotangent, 0, 1), own, s)
    t1 = jnp.pad(token_w1.astype(bf), ((0, pad), (0, 0)))
    t2 = jnp.pad(token_w2.astype(bf), ((0, 0), (0, pad)))
    tb1 = token_bias[:hidden, None]
    tb2 = jnp.pad(token_bias[hidden:], (0, pad))[:, None]

    chain = Chain()
    digits = bits_of(n_dp)
    halved, exchanged = digits[:2], digits[2:]
    flat = lambda a: a.reshape(own * s, c)
    images = lambda a: a.reshape(own, s, c)
    upper = {bit: upper_of("dp", bit).reshape(1).astype(jnp.int32) for bit in digits}
    swap_dp = lambda values, bit: swap(values, "dp", n_dp, bit)

    def sum_steps(a, b, bits):
        parts = a.v.shape[0]
        left = list(halved)
        for bit in bits:
            at = left.index(bit)
            rows = a.v.shape[0] * a.v.shape[1] // (2 ** (at + 1) * parts)
            view = lambda v: v.reshape(-1, 2, rows, c)
            chain.tie(b)
            keep, send = split_add(upper[bit], view(a.v), view(b.v))
            left.remove(bit)
            a = chain.mark(Box(keep))
            b = Box(swap_dp(send, bit))
            yield
        chain.tie(b)
        return chain.mark(Box(add(a.v, b.v).reshape(parts, -1, c)))

    def image_steps(part, near_first):
        far = Box(swap_mp(part.v, 2))
        yield
        if near_first:
            chain.tie(part)
            near = Box(swap_mp(part.v, 1))
            yield
            chain.end(near)
            yield
        chain.end(far)
        diag = Box(swap_mp(far.v, 1))
        if not near_first:
            chain.tie(part)
            near = Box(swap_mp(part.v, 1))
        yield
        chain.end(near)
        chain.end(diag)
        yield
        chain.tie(part)
        return chain.mark(Box(gather_images(order, [part.v, near.v, far.v, diag.v], s_true)))

    mixed, second, low, t_act, t_slope = token_fwd(row_weight, x, ct, t1.T, t2.T, tb1, tb2, vec_params)
    second = flat(second)
    low = flat(low)
    w_core = Box(w_core)
    w_x = Box(w_x)
    o0, q0, d0, e0 = (Box(v) for v in chan(second, low, w_own))
    chain.mark(o0)
    chain.tie(w_core)
    o1, q1, d1, e1 = (Box(v) for v in chan(second, low, w_core.v))
    chain.mark(o1)
    d1 = Box(swap_mp(d1.v, 1))
    chain.end(w_x)
    w_diag = Box(swap_mp(w_x.v, 1))
    o2, d2b, slope2 = (Box(v) for v in chan_fwd(second, low, w_x.v))
    chain.mark(o2)
    mine = Flow(sum_steps(d0, d1, halved))
    chain.tie(w_diag)
    out, d3b, slope3 = chan_last(second, low, w_diag.v, vec_params, [o0.v, o1.v, o2.v], flat(mixed))
    d3b = Box(swap_mp(d3b, 1))
    slope3 = Box(slope3)
    out = chain.mark(Box(images(out)))
    out = Flow(image_steps(out, False))
    chain.tie(slope3)
    q3, d3a, e3 = (Box(v) for v in chan_bwd(second, low, w_diag.v, slope3.v))
    chain.mark(q3)
    mine.go()

    def theirs_steps(part, near, far, bits):
        theirs = yield from sum_steps(near, far, bits)
        got = Box(swap_mp(theirs.v, 2))
        yield
        while not mine.ended:
            mine.go()
        chain.tie(got)
        piece = chain.mark(Box(add(mine.value.v[part], got.v[0])))
        for bit in exchanged:
            got = Box(swap_dp(piece.v, bit))
            yield
            chain.tie(got)
            piece = chain.mark(Box(add(piece.v, got.v)))
        piece = yield from gather_steps(chain, piece, "dp", n_dp, bits[:0:-1])
        got = Box(swap_dp(piece.v, bits[0]))
        yield
        chain.tie(got)
        weight, moments = ((chan_w1, chan_w1_moments), (chan_w2, chan_w2_moments))[part]
        new, moments = (Box(v) for v in update(part == 0, upper[bits[0]], piece.v, got.v, weight, moments))
        chain.mark(new)
        return new, moments

    lead = lambda box: Box(box.v[None])
    theirs2 = Flow(theirs_steps(1, lead(d2b), lead(d3b), halved))
    d3a = Box(swap_mp(d3a.v, 1))
    chain.tie(slope2)
    q2, d2a, e2 = (Box(v) for v in chan_bwd(second, low, w_x.v, slope2.v))
    chain.mark(q2)
    theirs1 = Flow(theirs_steps(0, lead(d2a), lead(d3a), halved[::-1]))
    mine.go()
    theirs2.go()
    chain.tie(q0)
    grads_of = [images(q.v) for q in (q0, q1, q2, q3)]
    ig, grads = token_bwd(row_weight, x, ct, mixed, grads_of, t_act, t_slope, t1, t2, vec_params)
    ig = chain.mark(Box(ig))

    shard_ids = jnp.arange(8)[:, None]
    b1_rows = sum(jnp.where(shard_ids == (j ^ m), e.v, 0.0) for m, e in enumerate((e0, e1, e2, e3)))
    small = jnp.concatenate([grads, b1_rows], axis=0)
    small = jnp.pad(small, ((0, -small.shape[0] % 32), (0, 0))).astype(bf)

    def small_steps(small):
        rows = small.shape[0]
        box = Box(small.reshape(2, rows // 2, c))
        box = yield from reduce_steps(chain, box, "mp", n_mp, [1])
        for axis, size, bit in [("mp", n_mp, 2)] + [("dp", n_dp, bit) for bit in digits]:
            got = Box(swap(box.v, axis, size, bit))
            yield
            chain.tie(got)
            box = chain.mark(Box(add(box.v, got.v)))
        box = yield from gather_steps(chain, box, "mp", n_mp, [1])
        return box.v.reshape(rows, c).astype(f32)

    def small_updates(small):
        token_w1_sum = small[:s_true, :hidden]
        token_w2_sum = small[:s_true, hidden : 2 * hidden].T
        vec_sum = small[s : s + 5]
        token_bias_sum = small[s + 5, : hidden + s_true]
        chan_b1_sum = lax.dynamic_slice_in_dim(small, s + 8 + j, 1, 0)[0]
        vec_moments_new = new_moments(vec_moments, vec_sum)
        token_w1_new, token_w1_moments_new = adam_update(token_w1, token_w1_moments, token_w1_sum)
        token_w2_new, token_w2_moments_new = adam_update(token_w2, token_w2_moments, token_w2_sum)
        token_bias_new, token_bias_moments_new = adam_update(token_bias, token_bias_moments, token_bias_sum)
        chan_b1_new, chan_b1_moments_new = adam_update(chan_b1, chan_b1_moments, chan_b1_sum)
        values = (
            vec_moments_new,
            token_w1_new,
            token_w1_moments_new,
            token_w2_new,
            token_w2_moments_new,
            token_bias_new,
            token_bias_moments_new,
            chan_b1_new,
            chan_b1_moments_new,
        )
        return [chain.end(Box(value)) for value in values]

    for flow in (theirs2, theirs1,):
        flow.go()
    small = Flow(small_steps(small))
    for flow in (out, small, theirs2, theirs1, out,):
        flow.go()
    ig = Flow(image_steps(chain.tie(ig), True))
    for flow in (ig, small, theirs1, out, ig, small, theirs2, theirs1, small, theirs2,):
        flow.go()
    while not small.ended:
        small.go()
    for flow in (theirs1, ig,):
        flow.go()
    while not small.ended:
        small.go()
    small = small_updates(small.value)
    for flow in (ig, ig, theirs2,):
        flow.go()
    for turn in range(3 * len(digits) + 9):
        for flow in (theirs2, theirs1):
            flow.go()
    output = out.value.v
    input_grad = ig.value.v
    chan_w1_new, chan_w1_moments_new = (box.v for box in theirs1.value)
    chan_w2_new, chan_w2_moments_new = (box.v for box in theirs2.value)

    (
        vec_moments_new,
        token_w1_new,
        token_w1_moments_new,
        token_w2_new,
        token_w2_moments_new,
        token_bias_new,
        token_bias_moments_new,
        chan_b1_new,
        chan_b1_moments_new,
    ) = (box.v for box in small)
    return (
        output,
        input_grad,
        vec_moments_new,
        token_w1_new,
        token_w1_moments_new,
        token_w2_new,
        token_w2_moments_new,
        token_bias_new,
        token_bias_moments_new,
        chan_w1_new,
        chan_w1_moments_new,
        chan_b1_new,
        chan_b1_moments_new,
        chan_w2_new,
        chan_w2_moments_new,
    )


def solution(mesh):
    placed = (
        P("dp", None, None),
        P("dp", None, None),
        P(),
        P(),
        P(),
        P(),
        P(),
        P(),
        P(),
        P(),
        P(),
        P(None, "mp"),
        P(None, None, "mp"),
        P("mp"),
        P(None, "mp"),
        P("mp", None),
        P(None, "mp", None),
    )
    return jax.shard_map(
        functools.partial(shards, mesh.shape["dp"]),
        mesh=mesh,
        in_specs=placed,
        out_specs=(
            P("dp", None, None),
            P("dp", None, None),
            P(),
            P(),
            P(),
            P(),
            P(),
            P(),
            P(),
            P(None, "mp"),
            P(None, None, "mp"),
            P("mp"),
            P(None, "mp"),
            P("mp", None),
            P(None, "mp", None),
        ),
        check_vma=False,
    )
```
